32 devices in a mesh: fsdp: 8 (over y, x, core), ep: 4 (over z).
Axes of the slice: x: 2, y: 2, z: 4, core: 2. Of those that a mesh axis runs over, the one named last changes fastest.
Arguments:
- hidden: bfloat16 [2048, 8192], P('fsdp', 'ep'), may hold values from -6 to 6
- w_down: bfloat16 [6144, 2, 8192], P('fsdp', None, 'ep'), may hold values from -0.0625 to 0.0625
- route_ids: int32 [1024, 2], P('fsdp'), may hold values from 0 to 7, as said below
- probs: float32 [1024, 2], P('fsdp'), may hold values from 0.1 to 0.9
- grad_out: bfloat16 [1024, 6144], P('fsdp', 'ep'), may hold values from -6 to 6
Outputs:
- output: bfloat16 [1024, 6144], P('fsdp', 'ep')
- grad_hidden: bfloat16 [2048, 8192], P('fsdp', 'ep')
- grad_weight: bfloat16 [6144, 2, 8192], P('fsdp', None, 'ep')
- grad_probs: float32 [1024, 2], P('fsdp')
The draws below stay inside these ranges and needn't reach their ends.
Inputs may be any that keep to these rules, and one draw needn't show every extreme that they name: `route_ids`: each token names 2 different experts. Within one panel's 128 tokens, experts 0 and 1 are each named by 1 to 128 tokens, and in some panel both are named by all 128 tokens.
All inputs are finite; a program needn't handle non-finite values.
Results may differ from the reference program's by a relative error of at most 0.012.
Values may be sent and summed in bfloat16 or wider, within the bound.
A program may use at most 384 MiB of HBM per device.

```python
import jax
import jax.numpy as jnp
from jax import lax

D = 6144
FF = 8192
EXPERTS = 8
EXP_WIN = 2
TOP = 2
BLOCK = 128
TOK_DEV = 128
NBLK = 2
ROWS = 256
TOKENS = 1024
N_FSDP = 8
N_EP = 4


def draw_route_ids(key, part):
    panels = TOKENS // TOK_DEV
    keys = jax.random.split(key, 7)
    counts = jax.random.randint(keys[0], (panels, 2), 1, TOK_DEV + 1)
    full_both = jax.random.randint(keys[1], (), 0, panels)
    counts = counts.at[full_both, 0].set(TOK_DEV).at[full_both, 1].set(TOK_DEV)
    order_keys = jax.random.split(keys[3], panels * 2)
    orders = jax.vmap(lambda single: jax.random.permutation(single, TOK_DEV))(order_keys).reshape(panels, 2, TOK_DEV)
    ranks = jnp.argsort(orders, axis=2)
    member = ranks < counts[:, :, None]
    in_zero = member[:, 0]
    in_one = member[:, 1]
    first_fill = jax.random.randint(keys[4], (panels, TOK_DEV), 2, EXPERTS)
    step_fill = jax.random.randint(keys[5], (panels, TOK_DEV), 1, EXPERTS - 2)
    second_fill = 2 + (first_fill - 2 + step_fill) % (EXPERTS - 2)
    flip = jax.random.randint(keys[6], (panels, TOK_DEV), 0, 2)
    first_pick = jnp.where(in_zero, 0, jnp.where(in_one, 1, first_fill))
    second_pick = jnp.where(in_zero & in_one, 1, jnp.where(in_zero | in_one, first_fill, second_fill))
    slot_first = jnp.where(flip == 1, second_pick, first_pick)
    slot_second = jnp.where(flip == 1, first_pick, second_pick)
    return jnp.stack([slot_first, slot_second], axis=2).reshape(TOKENS, 2).astype(jnp.int32)


def block_scale(own_key, extent, shards, least, largest):
    gain = 1.0
    for position, blocks in shards:
        draws = jax.random.uniform(jax.random.fold_in(jax.random.fold_in(own_key, 6), position), (blocks,), jnp.float32, least / len(shards), largest / len(shards))
        gain = gain * jnp.repeat(jnp.exp(draws), extent[position] // blocks).reshape((-1,) + (1,) * (len(extent) - 1 - position))
    return gain


def gaussian(rng, dims, width, reach, cuts=(), kind=jnp.bfloat16):
    array = width * jax.random.normal(rng, dims, jnp.float32)
    if cuts:
        array = array * block_scale(rng, dims, cuts, -0.22, 0.18)
    return jnp.clip(array, -reach, reach).astype(kind)


def setup_inputs(seed: int = 0) -> dict:
    seeds = jax.random.split(jax.random.key(seed), 6)
    hidden = gaussian(seeds[0], (N_FSDP * ROWS, FF), 1.0, 6.0, ((0, 8), (1, 4)))
    w_down = gaussian(seeds[1], (D, EXP_WIN, FF), FF ** -0.5, 0.0625, ((0, 8), (2, 4)))
    route_ids = draw_route_ids(jax.random.fold_in(seeds[5], 71), 0)
    probs = jnp.clip(0.1 + 0.79999997 * jax.random.uniform(seeds[3], (TOKENS, TOP), jnp.float32) ** block_scale(seeds[3], (TOKENS, TOP), ((0, 8),), -0.2, 0.2), 0.1, 0.9)
    grad_out = gaussian(seeds[4], (TOKENS, D), 1.0, 6.0, ((0, 8), (1, 4)))
    return {"hidden": hidden, "w_down": w_down, "route_ids": route_ids, "probs": probs, "grad_out": grad_out}


def route_layout(route_part, prob_part, expert_count, block_rows, row_count):
    token_count = route_part.shape[0]
    experts = jnp.arange(expert_count, dtype=jnp.int32)
    hits = (route_part[:, :, None] == experts[None, None, :]).astype(jnp.int32)
    named = jnp.sum(hits, axis=1).astype(jnp.int32)
    counts = jnp.sum(named, axis=0).astype(jnp.int32)
    ranks = (jnp.cumsum(named, axis=0) - named).astype(jnp.int32)
    padded = (((counts + block_rows - 1) // block_rows) * block_rows).astype(jnp.int32)
    offsets = (jnp.cumsum(padded) - padded).astype(jnp.int32)
    row_of = jnp.sum(hits * (offsets[None, None, :] + ranks[:, None, :]), axis=2).astype(jnp.int32)
    valid = jnp.sum(hits, axis=2).astype(jnp.int32)
    starts = jnp.arange(row_count // block_rows, dtype=jnp.int32) * block_rows
    inside = (starts[:, None] >= offsets[None, :]) & (starts[:, None] < (offsets + padded)[None, :])
    block_exp = (jnp.sum(jnp.where(inside, experts[None, :] + 1, 0), axis=1) - 1).astype(jnp.int32)
    target = jnp.where(valid > 0, row_of, row_count).reshape(-1).astype(jnp.int32)
    token_index = jnp.broadcast_to(jnp.arange(token_count, dtype=jnp.int32)[:, None], route_part.shape).reshape(-1)
    row_tok = jnp.zeros((row_count,), jnp.int32).at[target].set(token_index, mode="drop")
    row_live = jnp.zeros((row_count,), jnp.int32).at[target].set(jnp.ones_like(token_index), mode="drop")
    row_prob = jnp.zeros((row_count,), prob_part.dtype).at[target].set(prob_part.reshape(-1), mode="drop")
    return row_of, valid, block_exp, row_tok, row_live, row_prob


def reference(hidden, w_down, route_ids, probs, grad_out):
    model_width = w_down.shape[0]
    expert_count = w_down.shape[1]
    unit_count = w_down.shape[2]
    group = unit_count // N_EP
    hidden_all = hidden.reshape(N_FSDP, ROWS, unit_count)
    route_all = route_ids.reshape(N_FSDP, TOK_DEV, TOP)
    prob_all = probs.reshape(N_FSDP, TOK_DEV, TOP)
    grad_all = grad_out.reshape(N_FSDP, TOK_DEV, model_width)

    def panel(total, inputs):
        hid, route_part, prob_part, grad_part = inputs
        row_of, valid, block_exp, row_tok, row_live, row_prob = route_layout(route_part, prob_part, expert_count, BLOCK, ROWS)
        safe_exp = jnp.maximum(block_exp, 0)
        prob_valid = prob_part * valid.astype(prob_part.dtype)
        routed = jnp.where(row_live[:, None] > 0, grad_part[row_tok], jnp.zeros((), grad_part.dtype))
        scaled = (row_prob[:, None] * routed.astype(jnp.float32)).astype(jnp.bfloat16)
        hid_blocks = hid.reshape(NBLK, BLOCK, unit_count)
        routed_blocks = routed.reshape(NBLK, BLOCK, model_width)

        def one_group(index):
            hid_group = lax.dynamic_slice_in_dim(hid_blocks, index * group, group, 2)
            weight_group = lax.dynamic_slice_in_dim(w_down, index * group, group, 2)
            chosen = jnp.take(weight_group, safe_exp, axis=1).astype(jnp.float32)
            out_rows = jnp.einsum('bri,dbi->brd', hid_group.astype(jnp.float32), chosen).reshape(ROWS, model_width)
            part = jnp.sum(prob_valid[:, :, None] * out_rows[row_of], axis=1).astype(jnp.bfloat16)
            back = jnp.einsum('brd,dbi->bri', routed_blocks.astype(jnp.float32), chosen).reshape(ROWS, group)
            return part, back

        parts, backs = lax.map(one_group, jnp.arange(N_EP, dtype=jnp.int32))
        combined = jnp.sum(parts.astype(jnp.float32), axis=0).astype(jnp.bfloat16)
        hidden_back = jnp.transpose(backs, (1, 0, 2)).reshape(ROWS, unit_count)
        grad_hid = (row_prob[:, None] * hidden_back).astype(jnp.bfloat16)
        row_dot = jnp.sum(hid.astype(jnp.float32) * hidden_back, axis=1)
        grad_prob = valid.astype(row_dot.dtype) * row_dot[row_of]
        row_exp = jnp.repeat(block_exp, BLOCK)
        member = (row_exp[:, None] == jnp.arange(expert_count, dtype=jnp.int32)[None, :]).astype(jnp.float32)
        masked = hid.astype(jnp.float32)[:, None, :] * member[:, :, None]
        term = jnp.einsum('rd,rei->dei', scaled.astype(jnp.float32), masked).astype(jnp.bfloat16)
        return total + term.astype(jnp.float32), (combined, grad_hid, grad_prob)

    start = jnp.zeros((model_width, expert_count, unit_count), jnp.float32)
    total, (combined, grad_hid, grad_prob) = lax.scan(panel, start, (hidden_all, route_all, prob_all, grad_all))
    output = combined.reshape(N_FSDP * TOK_DEV, model_width)
    grad_hidden = grad_hid.reshape(N_FSDP * ROWS, unit_count)
    grad_probs = grad_prob.reshape(N_FSDP * TOK_DEV, TOP)
    return output, grad_hidden, total.astype(jnp.bfloat16), grad_probs
```

```python
import functools

import jax
import jax.numpy as jnp
from jax import lax
from jax.experimental import pallas as pl
from jax.experimental.layout import Layout, with_layout_constraint
from jax.experimental.pallas import tpu as pltpu
from jax.sharding import PartitionSpec as P

F32 = jnp.float32
BF16 = jnp.bfloat16
MESH = pl.DeviceIdType.MESH
VMEM = pl.BlockSpec(memory_space=pltpu.VMEM)


def meet(n_fsdp, n_ep, p, z):
    barrier = pltpu.get_barrier_semaphore()
    for s in range(1, n_ep):
        pl.semaphore_signal(
            barrier, inc=1, device_id=(p, lax.rem(z + s, n_ep)), device_id_type=MESH
        )
    for s in range(1, n_fsdp):
        pl.semaphore_signal(
            barrier, inc=1, device_id=(lax.rem(p + s, n_fsdp), z), device_id_type=MESH
        )
    pl.semaphore_wait(barrier, n_ep - 1 + n_fsdp - 1)


def remote(src, dst, send, recv, to):
    return pltpu.make_async_remote_copy(
        src_ref=src, dst_ref=dst, send_sem=send, recv_sem=recv, device_id=to, device_id_type=MESH
    )


def spread_kernel(
    n_fsdp, n_ep, g_ref, h_ref, out_ref, hall_ref, held, zsend, zrecv, psend, precv, hsend, fsend, hrecv, own
):
    ratio = g_ref.shape[0]
    n_chip = n_fsdp // 2
    p, z = lax.axis_index("fsdp"), lax.axis_index("ep")
    chip, core = lax.div(p, 2), lax.rem(p, 2)
    mate = chip * 2 + 1 - core
    meet(n_fsdp, n_ep, p, z)
    sends = []
    for s in range(1, n_ep):
        copy = remote(g_ref, held.at[z], zsend.at[s], zrecv.at[z], (p, lax.rem(z + s, n_ep)))
        copy.start()
        sends.append(copy)
    keep = pltpu.make_async_copy(h_ref, hall_ref.at[:, p], own)
    keep.start()

    def pieces(s, act):
        q = lax.rem(z + n_ep - s, n_ep)
        for r in range(ratio):
            block = held.at[q, r] if s else g_ref.at[r]
            i = q * ratio + r

            @pl.when(i != p)
            def _():
                act(remote(block, out_ref.at[p], psend.at[s, r], precv.at[p], (i, z)))

            if act is begin:

                @pl.when(i == p)
                def _():
                    out_ref[p] = block[...]

    def begin(copy):
        copy.start()

    def end(copy):
        copy.wait_send()

    pieces(0, begin)
    for s in range(1, n_chip):
        to = lax.rem(chip + s, n_chip) * 2 + core
        copy = remote(h_ref, hall_ref.at[:, p], hsend.at[s], hrecv.at[p], (to, z))
        copy.start()
        sends.append(copy)
    copy = remote(h_ref, hall_ref.at[:, p], hsend.at[0], hrecv.at[p], (mate, z))
    copy.start()
    sends.append(copy)
    for s in range(1, max(n_ep, n_chip)):
        if s < n_ep:
            q = lax.rem(z + n_ep - s, n_ep)
            remote(g_ref, held.at[q], zsend.at[s], zrecv.at[q], (p, z)).wait_recv()
            pieces(s, begin)
        if s < n_chip:
            f = lax.rem(chip + n_chip - s, n_chip) * 2 + core
            copy = remote(hall_ref.at[:, f], hall_ref.at[:, f], fsend.at[s], hrecv.at[f], (mate, z))
            copy.wait_recv()
            copy.start()
            sends.append(copy)
    for s in range(n_chip):
        f = lax.rem(chip + s, n_chip) * 2 + 1 - core
        remote(h_ref, hall_ref.at[:, f], hsend.at[0], hrecv.at[f], (mate, z)).wait_recv()
    for s in range(1, n_fsdp):
        f = lax.rem(p + s, n_fsdp)
        remote(g_ref.at[0], out_ref.at[f], psend.at[0, 0], precv.at[f], (f, z)).wait_recv()
    for s in range(n_ep):
        pieces(s, end)
    for copy in sends:
        copy.wait_send()
    keep.wait()


def collect_kernel(n_fsdp, n_ep, part_ref, out_ref, held, sums, psend, precv, zsend, zrecv):
    ratio = out_ref.shape[0]
    p, z = lax.axis_index("fsdp"), lax.axis_index("ep")
    meet(n_fsdp, n_ep, p, z)
    held[p] = part_ref[p]
    across = []
    for s in range(1, n_fsdp):
        i = lax.rem(p + s, n_fsdp)
        copy = remote(part_ref.at[i], held.at[p], psend.at[s], precv.at[p], (i, z))
        copy.start()
        across.append(copy)
    along = []
    for s in range(1, n_ep + 1):
        q = lax.rem(z + s, n_ep)
        for r in range(ratio):
            f = q * ratio + r

            @pl.when(f != p)
            def _():
                remote(part_ref.at[0], held.at[f], psend.at[0], precv.at[f], (p, z)).wait_recv()

        if s < n_ep:
            copy = remote(
                held.at[pl.ds(q * ratio, ratio)], sums.at[z], zsend.at[s], zrecv.at[z], (p, q)
            )
            copy.start()
            along.append(copy)
    total = held[pl.ds(z * ratio, ratio)].astype(F32)
    for s in range(1, n_ep):
        q = lax.rem(z + s, n_ep)
        remote(
            held.at[pl.ds(q * ratio, ratio)], sums.at[q], zsend.at[s], zrecv.at[q], (p, q)
        ).wait_recv()
        total = total + sums[q].astype(F32)
    out_ref[...] = total.astype(BF16)
    for copy in across + along:
        copy.wait_send()


def add_kernel(n_ep, x_ref, out_ref, held, send, recv):
    p, z = lax.axis_index("fsdp"), lax.axis_index("ep")
    meet(1, n_ep, p, z)
    copies = []
    for s in range(1, n_ep):
        copy = remote(x_ref, held.at[z], send.at[s], recv.at[z], (p, lax.rem(z + s, n_ep)))
        copy.start()
        copies.append(copy)
    total = x_ref[...]
    for s in range(1, n_ep):
        q = lax.rem(z + s, n_ep)
        remote(x_ref, held.at[q], send.at[s], recv.at[q], (p, q)).wait_recv()
        total = total + held[q]
    out_ref[...] = total
    for copy in copies:
        copy.wait_send()


def talk(body, key, x, shape, scratch, flops=0):
    return pl.pallas_call(
        body,
        out_shape=jax.ShapeDtypeStruct(shape, x.dtype),
        in_specs=[VMEM],
        out_specs=VMEM,
        scratch_shapes=scratch,
        cost_estimate=pl.CostEstimate(flops=flops, bytes_accessed=100_000_000, transcendentals=0),
        compiler_params=pltpu.CompilerParams(collective_id=key, has_side_effects=True),
    )(x)


def spread(grad_out, scaled, n_fsdp, n_ep):
    tokens, width = grad_out.shape
    experts, _, units = scaled.shape
    ratio = n_fsdp // n_ep
    cut = width // ratio
    blocks = jnp.stack([grad_out[:, r * cut : (r + 1) * cut] for r in range(ratio)])
    dma = pltpu.SemaphoreType.DMA
    anywhere = pl.BlockSpec(memory_space=pl.ANY)
    out, hid_all = pl.pallas_call(
        functools.partial(spread_kernel, n_fsdp, n_ep),
        out_shape=(
            jax.ShapeDtypeStruct((n_fsdp, tokens, cut), BF16),
            jax.ShapeDtypeStruct((experts, n_fsdp, tokens, units), BF16),
        ),
        in_specs=[VMEM, anywhere],
        out_specs=(VMEM, anywhere),
        scratch_shapes=[
            pltpu.VMEM((n_ep, ratio, tokens, cut), BF16),
            dma((n_ep,)),
            dma((n_ep,)),
            dma((n_ep, ratio)),
            dma((n_fsdp,)),
            dma((n_fsdp // 2,)),
            dma((n_fsdp // 2,)),
            dma((n_fsdp,)),
            dma,
        ],
        compiler_params=pltpu.CompilerParams(collective_id=0, has_side_effects=True),
    )(blocks, scaled)
    return out.reshape(n_fsdp * tokens, cut), hid_all.reshape(experts, n_fsdp * tokens, units)


def collect(part, n_fsdp, n_ep):
    cut = part.shape[1]
    tokens = part.shape[0] // n_fsdp
    ratio = n_fsdp // n_ep
    dma = pltpu.SemaphoreType.DMA
    out = talk(
        functools.partial(collect_kernel, n_fsdp, n_ep),
        1,
        part.reshape(n_fsdp, tokens, cut),
        (ratio, tokens, cut),
        [
            pltpu.VMEM((n_fsdp, tokens, cut), BF16),
            pltpu.VMEM((n_ep, ratio, tokens, cut), BF16),
            dma((n_fsdp,)),
            dma((n_fsdp,)),
            dma((n_ep,)),
            dma((n_ep,)),
        ],
    )
    return jnp.concatenate([out[r] for r in range(ratio)], axis=1)


def add_up(x, n_ep):
    dma = pltpu.SemaphoreType.DMA
    return talk(
        functools.partial(add_kernel, n_ep),
        2,
        x,
        x.shape,
        [pltpu.VMEM((n_ep,) + x.shape, F32), dma((n_ep,)), dma((n_ep,))],
    )


def route_maps(route_ids, probs, experts):
    tokens = route_ids.shape[0]
    names = jnp.arange(experts, dtype=jnp.int32)
    hits = (route_ids[:, :, None] == names[None, None, :]).astype(F32)
    named = jnp.sum(hits, axis=1)
    place = jnp.arange(tokens, dtype=jnp.int32)
    earlier = (place[None, :] < place[:, None]).astype(F32)
    rank = jnp.sum(earlier[:, :, None] * named[None, :, :], axis=1).astype(jnp.int32)
    token_prob = jnp.sum(hits * probs[:, :, None], axis=1)
    owns = (rank.T[:, :, None] == place[None, None, :]) & (named.T[:, :, None] > 0)
    return hits, token_prob, owns.astype(BF16)


def local(n_fsdp, n_ep, hidden, w_down, route_ids, probs, grad_out):
    rows, units = hidden.shape
    experts = w_down.shape[1]
    tokens = route_ids.shape[0]
    hits, token_prob, owns = route_maps(route_ids, probs, experts)
    hid_tok = jnp.einsum(
        "etr,erf->etf", owns, hidden.reshape(experts, tokens, units), preferred_element_type=F32
    )
    scaled = (token_prob.T[:, :, None] * hid_tok).astype(BF16)
    hid_tok = hid_tok.astype(BF16)
    grads, hid_all = spread(grad_out, scaled, n_fsdp, n_ep)
    back_part = jnp.einsum("td,def->tef", grads, w_down, preferred_element_type=F32).astype(BF16)
    hid_all, back_part = lax.optimization_barrier((hid_all, back_part))
    back = lax.psum_scatter(back_part, "fsdp", scatter_dimension=0, tiled=True)
    part = jnp.einsum("etf,def->td", hid_all, w_down, preferred_element_type=F32).astype(BF16)
    output = collect(part, n_fsdp, n_ep)
    grad_weight = jnp.einsum("td,etf->def", grads, hid_all, preferred_element_type=F32).astype(BF16)
    grad_weight = with_layout_constraint(grad_weight, Layout(major_to_minor=(0, 1, 2)))
    back, output, grad_weight = lax.optimization_barrier((back, output, grad_weight))
    back = back.astype(F32)
    dots = jnp.sum(hid_tok.transpose(1, 0, 2).astype(F32) * back, axis=2)
    dots = add_up(dots.T, n_ep).T
    grad_tok = (token_prob[:, :, None] * back).astype(BF16)
    grad_hidden = jnp.einsum("etr,tef->erf", owns, grad_tok, preferred_element_type=F32)
    grad_hidden = grad_hidden.astype(BF16).reshape(rows, units)
    grad_probs = jnp.sum(hits * dots[:, None, :], axis=2)
    return (output, grad_hidden, grad_weight, grad_probs)


NT = (((1,), (1,)), ((), ()))
NN = (((1,), (0,)), ((), ()))
TN = (((0,), (0,)), ((), ()))


def dot(a, b, dims):
    return lax.dot_general(a, b, dims, preferred_element_type=F32)


def fused_kernel(
    g_ref, s_ref, h_ref, own_ref, tp_ref, w_ref,
    out_ref, gh_ref, gw_ref, dots_ref,
    wst, wall, hall, gz, gall, gmate, op, oz, oz2, os2, osum, orow, ofin, bp, rx, ry, sx, sy, r2x, r2y, gtok, dt, dmine, dz,
    wsem, hsem, gwsem,
    wss, wsr, hxs, hxr, hys, hyr, h2s, h2r, hms, hmr, g1s, g1r, g2s, g2r, g3s, g3r, gms, gmr,
    ozs, ozr, o2s, o2r, oas, oar, obs, obr, bxs, bxr, bys, byr, cxs, cxr, cys, cyr, ds_, dr_,
):
    p, z = lax.axis_index("fsdp"), lax.axis_index("ep")
    k, c = lax.rem(p, 2), lax.div(p, 2)
    x, y = lax.rem(c, 2), lax.div(c, 2)
    lo, hi = lax.rem(z, 2), lax.div(z, 2)
    xn, yn = c + 1 - 2 * x, c + 2 - 4 * y
    dg = yn + 1 - 2 * x
    z1, z2 = z + 1 - 2 * lo, z + 2 - 4 * hi
    z3 = z2 + 1 - 2 * lo
    zs = (z, z1, z2, z3)
    chips = (c, xn, yn, dg)
    width = gmate.shape[3]
    half = s_ref.shape[2] // 2
    sub = gz.shape[1]
    mate = (c * 2 + 1 - k, z)
    to_x, to_y, to_d = (xn * 2 + k, z), (yn * 2 + k, z), (dg * 2 + k, z)
    to_z = (None, (p, z1), (p, z2), (p, z3))
    mine = pl.multiple_of(k * width, 128)
    other = pl.multiple_of((1 - k) * width, 128)
    halves = (pl.ds(0, half), pl.ds(half, half))
    sends = []

    def put(src, dst, ssem, rsem, to):
        copy = remote(src, dst, ssem, rsem, to)
        copy.start()
        sends.append(copy)

    def got(dst, ssem, rsem):
        remote(dst, dst, ssem, rsem, mate).wait_recv()

    n_w = wsem.shape[0]
    rows_w = width // n_w
    loads = []
    for i in range(n_w):
        rows = pl.ds(i * rows_w, rows_w)
        copy = pltpu.make_async_copy(w_ref.at[rows], wst.at[rows], wsem.at[i])
        copy.start()
        loads.append(copy)
    keep = pltpu.make_async_copy(s_ref, hall.at[:, k, c], hsem)
    keep.start()

    barrier = pltpu.get_barrier_semaphore()
    partners = [mate, to_x, to_y, to_d, to_z[1], to_z[2], to_z[3]]
    partners += [(q * 2 + 1 - k, z) for q in (xn, yn, dg)]
    for to in partners:
        pl.semaphore_signal(barrier, inc=1, device_id=to, device_id_type=MESH)
    pl.semaphore_wait(barrier, len(partners))

    for s in (1, 2, 3):
        put(g_ref.at[pl.ds(zs[s] * sub, sub)], gz.at[z], g1s.at[s], g1r.at[s], to_z[s])
    for e in range(2):
        put(s_ref.at[e, :, halves[0]], hall.at[e, k, c, :, halves[0]], hxs.at[e], hxr.at[e], to_x)
        put(s_ref.at[e, :, halves[1]], hall.at[e, k, c, :, halves[1]], hys.at[e], hyr.at[e], to_y)
    put(s_ref, hall.at[:, k, c], hms.at[0], hmr.at[0], mate)
    gz[z] = g_ref[pl.ds(z * sub, sub)]

    r = lax.broadcasted_iota(jnp.int32, (rows_w, 2 * rows_w), 0)
    q = lax.broadcasted_iota(jnp.int32, (rows_w, 2 * rows_w), 1)
    picks = [(q == 2 * r + e).astype(BF16) for e in range(2)]
    for i in range(n_w):
        loads[i].wait()
        block = wst[pl.ds(i * rows_w, rows_w)].reshape(2 * rows_w, 2 * half)
        rows = pl.ds(mine + i * rows_w, rows_w)
        for e in range(2):
            wall[e, rows] = dot(picks[e], block, NN).astype(BF16)
        put(wall.at[:, rows], wall.at[:, rows], wss.at[i], wsr.at[i], mate)

    def product(g):
        ci = chips[g]
        acc = jnp.zeros((2 * 4 * sub, width), F32)
        for e in range(2):
            acc += dot(hall[e, :, ci].reshape(2 * 4 * sub, 2 * half), wall[e, pl.ds(mine, width)], NT)
        op[g] = acc.astype(BF16).reshape(2, 2, 2, sub, width)
        put(op.at[g, :, :, 1 - lo], oz.at[g], ozs.at[g], ozr.at[g], to_z[1])

    def relay(g):
        got(oz.at[g], ozs.at[g], ozr.at[g])
        os2[g] = (op[g, :, 1 - hi, lo].astype(F32) + oz[g, :, 1 - hi].astype(F32)).astype(BF16)
        put(os2.at[g], oz2.at[g], o2s.at[g], o2r.at[g], to_z[2])

    def back(s):
        lhs = gall[:, zs[s]].reshape(4 * sub, 2 * width)
        for e in range(2):

            def tile(t, _):
                cols = pl.ds(pl.multiple_of(t * half, 128), half)
                acc = dot(lhs, wall[e, :, cols], NN)
                bp[s, e, :, :, :, cols] = acc.astype(BF16).reshape(2, 2, sub, half)
                return 0

            lax.fori_loop(0, 2, tile, 0)
        put(bp.at[s, :, :, 1 - x, :, halves[0]], rx.at[s], bxs.at[s], bxr.at[s], to_x)
        put(bp.at[s, :, 1 - y, :, :, halves[1]], ry.at[s], bys.at[s], byr.at[s], to_y)

    def turn(s):
        got(rx.at[s], bxs.at[s], bxr.at[s])
        sy[s] = (bp[s, :, 1 - y, x, :, halves[0]].astype(F32) + rx[s, :, 1 - y].astype(F32)).astype(BF16)
        put(sy.at[s], r2y.at[s], cys.at[s], cyr.at[s], to_y)
        got(ry.at[s], bys.at[s], byr.at[s])
        sx[s] = (bp[s, :, y, 1 - x, :, halves[1]].astype(F32) + ry[s, :, 1 - x].astype(F32)).astype(BF16)
        put(sx.at[s], r2x.at[s], cxs.at[s], cxr.at[s], to_x)

    def settle(s):
        got(r2y.at[s], cys.at[s], cyr.at[s])
        got(r2x.at[s], cxs.at[s], cxr.at[s])
        rows = pl.ds(pl.multiple_of(zs[s] * sub, sub), sub)
        for e in range(2):
            total = jnp.zeros((sub, 1), F32)
            for b in range(2):
                if b == 0:
                    value = rx[s, e, y].astype(F32) + r2y[s, e].astype(F32)
                else:
                    value = ry[s, e, x].astype(F32) + r2x[s, e].astype(F32)
                value += bp[s, e, y, x, :, halves[b]].astype(F32)
                gtok[e, rows, halves[b]] = (tp_ref[e, rows] * value).astype(BF16)
                total += jnp.sum(h_ref[e, rows, halves[b]].astype(F32) * value, axis=1, keepdims=True)
            dt[e, rows] = jnp.broadcast_to(total, (sub, 128))

    n_g = gwsem.shape[0]
    rows_g = width // n_g
    stores = []

    def weight(i):
        rows = pl.ds(i * rows_g, rows_g)
        for e in range(2):

            def tile(t, _):
                cols = pl.ds(pl.multiple_of(t * half, 128), half)
                acc = dot(
                    gall[:, :, :, pl.ds(pl.multiple_of(mine + i * rows_g, 128), rows_g)].reshape(16 * sub, rows_g),
                    hall[e, k, :, :, cols].reshape(16 * sub, half),
                    TN,
                )
                acc += dot(
                    gmate[:, :, :, rows].reshape(16 * sub, rows_g),
                    hall[e, 1 - k, :, :, cols].reshape(16 * sub, half),
                    TN,
                )
                wst[rows, e, cols] = acc.astype(BF16)
                return 0

            lax.fori_loop(0, 2, tile, 0)
        copy = pltpu.make_async_copy(wst.at[rows], gw_ref.at[rows], gwsem.at[i])
        copy.start()
        stores.append(copy)

    def share(s):
        j = zs[s]
        put(gall.at[:, j, :, pl.ds(other, width)], gmate.at[:, j], gms.at[s], gmr.at[s], mate)

    keep.wait()
    got(hall.at[:, 1 - k, c], hms.at[0], hmr.at[0])
    product(0)

    for s in (1, 2, 3):
        got(gz.at[zs[s]], g1s.at[s], g1r.at[s])
    for i, to in ((1, to_x), (2, to_y), (3, to_d)):
        put(gz.at[chips[i]], gall.at[c, z], g2s.at[i], g2r.at[i], to)
    gall[c, z] = gz[c]
    for e in range(2):
        put(s_ref.at[e, :, halves[1]], hall.at[e, k, c, :, halves[1]], hxs.at[2 + e], hxr.at[2 + e], to_x)
        put(s_ref.at[e, :, halves[0]], hall.at[e, k, c, :, halves[0]], hys.at[2 + e], hyr.at[2 + e], to_y)
    for e in range(2):
        block = hall.at[e, k, xn, :, halves[0]]
        got(block, hxs.at[e], hxr.at[e])
        put(block, block, h2s.at[e], h2r.at[e], to_y)
        block = hall.at[e, k, yn, :, halves[1]]
        got(block, hys.at[e], hyr.at[e])
        put(block, block, h2s.at[2 + e], h2r.at[2 + e], to_x)
    for i in (1, 2, 3):
        got(gall.at[chips[i], z], g2s.at[i], g2r.at[i])
    put(gall.at[:, z], gall.at[:, z], g3s.at[2], g3r.at[2], to_z[2])
    put(gall.at[:, z], gall.at[:, z], g3s.at[1], g3r.at[1], to_z[1])
    share(0)
    for i in range(n_w):
        rows = pl.ds(other + i * rows_w, rows_w)
        got(wall.at[:, rows], wss.at[i], wsr.at[i])
    back(0)
    relay(0)
    got(gall.at[:, z2], g3s.at[2], g3r.at[2])
    put(gall.at[:, z2], gall.at[:, z2], g3s.at[3], g3r.at[3], to_z[1])
    share(2)
    turn(0)
    back(2)
    for e in range(2):
        got(hall.at[e, k, xn, :, halves[1]], hxs.at[2 + e], hxr.at[2 + e])
    put(hall.at[:, k, xn], hall.at[:, k, xn], hms.at[1], hmr.at[1], mate)
    for e in range(2):
        got(hall.at[e, k, yn, :, halves[0]], hys.at[2 + e], hyr.at[2 + e])
    put(hall.at[:, k, yn], hall.at[:, k, yn], hms.at[2], hmr.at[2], mate)
    got(hall.at[:, 1 - k, xn], hms.at[1], hmr.at[1])
    product(1)
    got(hall.at[:, 1 - k, yn], hms.at[2], hmr.at[2])
    product(2)
    got(gall.at[:, z1], g3s.at[1], g3r.at[1])
    share(1)
    back(1)
    turn(2)
    relay(1)
    relay(2)
    for e in range(2):
        got(hall.at[e, k, dg, :, halves[0]], h2s.at[e], h2r.at[e])
        got(hall.at[e, k, dg, :, halves[1]], h2s.at[2 + e], h2r.at[2 + e])
    put(hall.at[:, k, dg], hall.at[:, k, dg], hms.at[3], hmr.at[3], mate)
    got(gall.at[:, z3], g3s.at[3], g3r.at[3])
    share(3)
    back(3)
    turn(1)
    got(hall.at[:, 1 - k, dg], hms.at[3], hmr.at[3])
    product(3)
    settle(0)
    for s in range(4):
        got(gmate.at[:, zs[s]], gms.at[s], gmr.at[s])
    weight(0)
    relay(3)
    turn(3)
    settle(2)
    for g in range(4):
        got(oz2.at[g], o2s.at[g], o2r.at[g])
        osum[g] = (
            op[g, :, hi, lo].astype(F32) + oz[g, :, hi].astype(F32) + oz2[g].astype(F32)
        ).astype(BF16)
    for g in range(4):
        for b in range(2):
            if g or b:
                put(osum.at[g, b_core(k, b)], orow.at[c, k], oas.at[g, b], oar.at[g, b], (chips[g] * 2 + b_core(k, b), z))
    orow[c, k] = osum[0, k]
    weight(1)
    for g in range(4):
        for b in range(2):
            if g or b:
                got(orow.at[chips[g], b_core(k, b)], oas.at[g, b], oar.at[g, b])
    for s in (1, 2, 3):
        put(orow.at[zs[s]], ofin.at[z], obs.at[s], obr.at[s], to_z[s])
    ofin[z] = orow[z]
    weight(2)
    settle(1)
    for s in (1, 2, 3):
        got(ofin.at[zs[s]], obs.at[s], obr.at[s])
    for j in range(4):
        for b in range(2):
            out_ref[pl.ds(j * sub, sub), pl.ds(b * width, width)] = ofin[j, b]
    settle(3)
    lane = lax.broadcasted_iota(jnp.int32, (4 * sub, 128), 1)
    both = jnp.where(lane == 0, dt[0], jnp.where(lane == 1, dt[1], 0.0))
    dmine[...] = both.T[0:8]
    for s in (1, 2, 3):
        put(dmine, dz.at[s], ds_.at[s], dr_.at[s], to_z[s])
    for e in range(2):
        gh_ref[e] = dot(own_ref[e], gtok[e], TN).astype(BF16)
    total = dmine[...]
    for s in (1, 2, 3):
        got(dz.at[s], ds_.at[s], dr_.at[s])
        total = total + dz[s]
    dots_ref[...] = total
    for copy in sends:
        copy.wait_send()
    for copy in stores:
        copy.wait()


def b_core(k, b):
    return 1 - k if b else k


def fused(grad_out, scaled, hid_tok, owns, token_prob, w_down):
    tokens = grad_out.shape[0]
    width, _, units = w_down.shape
    sub = tokens // 4
    half = units // 2
    dma = pltpu.SemaphoreType.DMA
    vmem = lambda *shape: pltpu.VMEM(shape, BF16)
    anywhere = pl.BlockSpec(memory_space=pl.ANY)
    pair = lambda *n: [dma(n), dma(n)]
    scratch = [
        vmem(width, 2, units),
        vmem(2, 2 * width, units),
        vmem(2, 2, 4, tokens, units),
        vmem(4, sub, 2 * width),
        vmem(4, 4, sub, 2 * width),
        vmem(4, 4, sub, width),
        vmem(4, 2, 2, 2, sub, width),
        vmem(4, 2, 2, sub, width),
        vmem(4, 2, sub, width),
        vmem(4, 2, sub, width),
        vmem(4, 2, sub, width),
        vmem(4, 2, sub, width),
        vmem(4, 2, sub, width),
        vmem(4, 2, 2, 2, sub, units),
        vmem(4, 2, 2, sub, half),
        vmem(4, 2, 2, sub, half),
        vmem(4, 2, sub, half),
        vmem(4, 2, sub, half),
        vmem(4, 2, sub, half),
        vmem(4, 2, sub, half),
        vmem(2, tokens, units),
        pltpu.VMEM((2, tokens, 128), F32),
        pltpu.VMEM((8, 128), F32),
        pltpu.VMEM((4, 8, 128), F32),
        dma((6,)),
        dma,
        dma((3,)),
    ]
    for n in ((6,), (4,), (4,), (4,), (4,), (4,), (4,), (4,), (4,), (4,), (4,), (4, 2), (4,), (4,), (4,), (4,), (4,), (4,)):
        scratch += pair(*n)
    return pl.pallas_call(
        fused_kernel,
        out_shape=(
            jax.ShapeDtypeStruct((tokens, 2 * width), BF16),
            jax.ShapeDtypeStruct((2, tokens, units), BF16),
            jax.ShapeDtypeStruct((width, 2, units), BF16),
            jax.ShapeDtypeStruct((8, 128), F32),
        ),
        in_specs=[VMEM] * 5 + [anywhere],
        out_specs=(VMEM, VMEM, anywhere, VMEM),
        scratch_shapes=scratch,
        compiler_params=pltpu.CompilerParams(
            collective_id=3, has_side_effects=True, vmem_limit_bytes=60 * 2**20
        ),
    )(grad_out, scaled, hid_tok, owns, token_prob, w_down)


def local_fused(hidden, w_down, route_ids, probs, grad_out):
    rows, units = hidden.shape
    experts = w_down.shape[1]
    tokens = route_ids.shape[0]
    hits, token_prob, owns = route_maps(route_ids, probs, experts)
    hid_tok = jnp.einsum(
        "etr,erf->etf", owns, hidden.reshape(experts, tokens, units), preferred_element_type=F32
    )
    scaled = (token_prob.T[:, :, None] * hid_tok).astype(BF16)
    hid_tok = hid_tok.astype(BF16)
    output, grad_hidden, grad_weight, dots = fused(
        grad_out, scaled, hid_tok, owns, token_prob.T[:, :, None], w_down
    )
    grad_probs = jnp.sum(hits * dots[:experts].T[:, None, :], axis=2)
    return (output, grad_hidden.reshape(rows, units), grad_weight, grad_probs)


def solution(mesh):
    placed = (
        P("fsdp", "ep"),
        P("fsdp", None, "ep"),
        P("fsdp", None),
        P("fsdp", None),
        P("fsdp", "ep"),
    )
    n_fsdp, n_ep = mesh.shape["fsdp"], mesh.shape["ep"]
    if (n_fsdp, n_ep) == (8, 4):
        body = local_fused
    else:
        body = functools.partial(local, n_fsdp, n_ep)
    return jax.shard_map(
        body,
        mesh=mesh,
        in_specs=placed,
        out_specs=(P("fsdp", "ep"), P("fsdp", "ep"), P("fsdp", None, "ep"), P("fsdp", None)),
        check_vma=False,
    )
```

```python
import functools

import jax
import jax.numpy as jnp
from jax import lax
from jax.experimental import pallas as pl
from jax.experimental.layout import Layout, with_layout_constraint
from jax.experimental.pallas import tpu as pltpu
from jax.sharding import PartitionSpec as P

F32 = jnp.float32
BF16 = jnp.bfloat16
MESH = pl.DeviceIdType.MESH
VMEM = pl.BlockSpec(memory_space=pltpu.VMEM)
VMEM_LIMIT = 50 * 2**20
FINISH_PARTS = 6


def meet(n_fsdp, n_ep, p, z):
    barrier = pltpu.get_barrier_semaphore()
    for s in range(1, n_ep):
        pl.semaphore_signal(
            barrier, inc=1, device_id=(p, lax.rem(z + s, n_ep)), device_id_type=MESH
        )
    for s in range(1, n_fsdp):
        pl.semaphore_signal(
            barrier, inc=1, device_id=(lax.rem(p + s, n_fsdp), z), device_id_type=MESH
        )
    pl.semaphore_wait(barrier, n_ep - 1 + n_fsdp - 1)


def remote(src, dst, send, recv, to):
    return pltpu.make_async_remote_copy(
        src_ref=src, dst_ref=dst, send_sem=send, recv_sem=recv, device_id=to, device_id_type=MESH
    )


def spread_kernel(
    n_fsdp, n_ep, g_ref, h_ref, out_ref, hall_ref, held, zsend, zrecv, psend, precv, hsend, fsend, hrecv, own
):
    ratio = g_ref.shape[0]
    n_chip = n_fsdp // 2
    p, z = lax.axis_index("fsdp"), lax.axis_index("ep")
    chip, core = lax.div(p, 2), lax.rem(p, 2)
    mate = chip * 2 + 1 - core
    meet(n_fsdp, n_ep, p, z)
    sends = []
    for s in range(1, n_ep):
        copy = remote(g_ref, held.at[z], zsend.at[s], zrecv.at[z], (p, lax.rem(z + s, n_ep)))
        copy.start()
        sends.append(copy)
    keep = pltpu.make_async_copy(h_ref, hall_ref.at[:, p], own)
    keep.start()

    def pieces(s, act):
        q = lax.rem(z + n_ep - s, n_ep)
        for r in range(ratio):
            block = held.at[q, r] if s else g_ref.at[r]
            i = q * ratio + r

            @pl.when(i != p)
            def _():
                act(remote(block, out_ref.at[p], psend.at[s, r], precv.at[p], (i, z)))

            if act is begin:

                @pl.when(i == p)
                def _():
                    out_ref[p] = block[...]

    def begin(copy):
        copy.start()

    def end(copy):
        copy.wait_send()

    pieces(0, begin)
    for s in range(1, n_chip):
        to = lax.rem(chip + s, n_chip) * 2 + core
        copy = remote(h_ref, hall_ref.at[:, p], hsend.at[s], hrecv.at[p], (to, z))
        copy.start()
        sends.append(copy)
    copy = remote(h_ref, hall_ref.at[:, p], hsend.at[0], hrecv.at[p], (mate, z))
    copy.start()
    sends.append(copy)
    for s in range(1, max(n_ep, n_chip)):
        if s < n_ep:
            q = lax.rem(z + n_ep - s, n_ep)
            remote(g_ref, held.at[q], zsend.at[s], zrecv.at[q], (p, z)).wait_recv()
            pieces(s, begin)
        if s < n_chip:
            f = lax.rem(chip + n_chip - s, n_chip) * 2 + core
            copy = remote(hall_ref.at[:, f], hall_ref.at[:, f], fsend.at[s], hrecv.at[f], (mate, z))
            copy.wait_recv()
            copy.start()
            sends.append(copy)
    for s in range(n_chip):
        f = lax.rem(chip + s, n_chip) * 2 + 1 - core
        remote(h_ref, hall_ref.at[:, f], hsend.at[0], hrecv.at[f], (mate, z)).wait_recv()
    for s in range(1, n_fsdp):
        f = lax.rem(p + s, n_fsdp)
        remote(g_ref.at[0], out_ref.at[f], psend.at[0, 0], precv.at[f], (f, z)).wait_recv()
    for s in range(n_ep):
        pieces(s, end)
    for copy in sends:
        copy.wait_send()
    keep.wait()


def collect_kernel(n_fsdp, n_ep, part_ref, out_ref, held, sums, psend, precv, zsend, zrecv):
    ratio = out_ref.shape[0]
    p, z = lax.axis_index("fsdp"), lax.axis_index("ep")
    meet(n_fsdp, n_ep, p, z)
    held[p] = part_ref[p]
    across = []
    for s in range(1, n_fsdp):
        i = lax.rem(p + s, n_fsdp)
        copy = remote(part_ref.at[i], held.at[p], psend.at[s], precv.at[p], (i, z))
        copy.start()
        across.append(copy)
    along = []
    for s in range(1, n_ep + 1):
        q = lax.rem(z + s, n_ep)
        for r in range(ratio):
            f = q * ratio + r

            @pl.when(f != p)
            def _():
                remote(part_ref.at[0], held.at[f], psend.at[0], precv.at[f], (p, z)).wait_recv()

        if s < n_ep:
            copy = remote(
                held.at[pl.ds(q * ratio, ratio)], sums.at[z], zsend.at[s], zrecv.at[z], (p, q)
            )
            copy.start()
            along.append(copy)
    total = held[pl.ds(z * ratio, ratio)].astype(F32)
    for s in range(1, n_ep):
        q = lax.rem(z + s, n_ep)
        remote(
            held.at[pl.ds(q * ratio, ratio)], sums.at[q], zsend.at[s], zrecv.at[q], (p, q)
        ).wait_recv()
        total = total + sums[q].astype(F32)
    out_ref[...] = total.astype(BF16)
    for copy in across + along:
        copy.wait_send()


def add_kernel(n_ep, x_ref, out_ref, held, send, recv):
    p, z = lax.axis_index("fsdp"), lax.axis_index("ep")
    meet(1, n_ep, p, z)
    copies = []
    for s in range(1, n_ep):
        copy = remote(x_ref, held.at[z], send.at[s], recv.at[z], (p, lax.rem(z + s, n_ep)))
        copy.start()
        copies.append(copy)
    total = x_ref[...]
    for s in range(1, n_ep):
        q = lax.rem(z + s, n_ep)
        remote(x_ref, held.at[q], send.at[s], recv.at[q], (p, q)).wait_recv()
        total = total + held[q]
    out_ref[...] = total
    for copy in copies:
        copy.wait_send()


def talk(body, key, x, shape, scratch, flops=0):
    return pl.pallas_call(
        body,
        out_shape=jax.ShapeDtypeStruct(shape, x.dtype),
        in_specs=[VMEM],
        out_specs=VMEM,
        scratch_shapes=scratch,
        cost_estimate=pl.CostEstimate(flops=flops, bytes_accessed=100_000_000, transcendentals=0),
        compiler_params=pltpu.CompilerParams(collective_id=key, has_side_effects=True),
    )(x)


def spread(grad_out, scaled, n_fsdp, n_ep):
    tokens, width = grad_out.shape
    experts, _, units = scaled.shape
    ratio = n_fsdp // n_ep
    cut = width // ratio
    blocks = jnp.stack([grad_out[:, r * cut : (r + 1) * cut] for r in range(ratio)])
    dma = pltpu.SemaphoreType.DMA
    anywhere = pl.BlockSpec(memory_space=pl.ANY)
    out, hid_all = pl.pallas_call(
        functools.partial(spread_kernel, n_fsdp, n_ep),
        out_shape=(
            jax.ShapeDtypeStruct((n_fsdp, tokens, cut), BF16),
            jax.ShapeDtypeStruct((experts, n_fsdp, tokens, units), BF16),
        ),
        in_specs=[VMEM, anywhere],
        out_specs=(VMEM, anywhere),
        scratch_shapes=[
            pltpu.VMEM((n_ep, ratio, tokens, cut), BF16),
            dma((n_ep,)),
            dma((n_ep,)),
            dma((n_ep, ratio)),
            dma((n_fsdp,)),
            dma((n_fsdp // 2,)),
            dma((n_fsdp // 2,)),
            dma((n_fsdp,)),
            dma,
        ],
        compiler_params=pltpu.CompilerParams(collective_id=0, has_side_effects=True),
    )(blocks, scaled)
    return out.reshape(n_fsdp * tokens, cut), hid_all.reshape(experts, n_fsdp * tokens, units)


def collect(part, n_fsdp, n_ep):
    cut = part.shape[1]
    tokens = part.shape[0] // n_fsdp
    ratio = n_fsdp // n_ep
    dma = pltpu.SemaphoreType.DMA
    out = talk(
        functools.partial(collect_kernel, n_fsdp, n_ep),
        1,
        part.reshape(n_fsdp, tokens, cut),
        (ratio, tokens, cut),
        [
            pltpu.VMEM((n_fsdp, tokens, cut), BF16),
            pltpu.VMEM((n_ep, ratio, tokens, cut), BF16),
            dma((n_fsdp,)),
            dma((n_fsdp,)),
            dma((n_ep,)),
            dma((n_ep,)),
        ],
    )
    return jnp.concatenate([out[r] for r in range(ratio)], axis=1)


def add_up(x, n_ep):
    dma = pltpu.SemaphoreType.DMA
    return talk(
        functools.partial(add_kernel, n_ep),
        2,
        x,
        x.shape,
        [pltpu.VMEM((n_ep,) + x.shape, F32), dma((n_ep,)), dma((n_ep,))],
    )


def route_maps(route_ids, probs, experts):
    tokens = route_ids.shape[0]
    names = jnp.arange(experts, dtype=jnp.int32)
    hits = (route_ids[:, :, None] == names[None, None, :]).astype(F32)
    named = jnp.sum(hits, axis=1)
    place = jnp.arange(tokens, dtype=jnp.int32)
    earlier = (place[None, :] < place[:, None]).astype(F32)
    rank = jnp.sum(earlier[:, :, None] * named[None, :, :], axis=1).astype(jnp.int32)
    token_prob = jnp.sum(hits * probs[:, :, None], axis=1)
    owns = (rank.T[:, :, None] == place[None, None, :]) & (named.T[:, :, None] > 0)
    return hits, token_prob, owns.astype(BF16)


def local(n_fsdp, n_ep, hidden, w_down, route_ids, probs, grad_out):
    rows, units = hidden.shape
    experts = w_down.shape[1]
    tokens = route_ids.shape[0]
    hits, token_prob, owns = route_maps(route_ids, probs, experts)
    hid_tok = jnp.einsum(
        "etr,erf->etf", owns, hidden.reshape(experts, tokens, units), preferred_element_type=F32
    )
    scaled = (token_prob.T[:, :, None] * hid_tok).astype(BF16)
    hid_tok = hid_tok.astype(BF16)
    grads, hid_all = spread(grad_out, scaled, n_fsdp, n_ep)
    back_part = jnp.einsum("td,def->tef", grads, w_down, preferred_element_type=F32).astype(BF16)
    hid_all, back_part = lax.optimization_barrier((hid_all, back_part))
    back = lax.psum_scatter(back_part, "fsdp", scatter_dimension=0, tiled=True)
    part = jnp.einsum("etf,def->td", hid_all, w_down, preferred_element_type=F32).astype(BF16)
    output = collect(part, n_fsdp, n_ep)
    grad_weight = jnp.einsum("td,etf->def", grads, hid_all, preferred_element_type=F32).astype(BF16)
    grad_weight = with_layout_constraint(grad_weight, Layout(major_to_minor=(0, 1, 2)))
    back, output, grad_weight = lax.optimization_barrier((back, output, grad_weight))
    back = back.astype(F32)
    dots = jnp.sum(hid_tok.transpose(1, 0, 2).astype(F32) * back, axis=2)
    dots = add_up(dots.T, n_ep).T
    grad_tok = (token_prob[:, :, None] * back).astype(BF16)
    grad_hidden = jnp.einsum("etr,tef->erf", owns, grad_tok, preferred_element_type=F32)
    grad_hidden = grad_hidden.astype(BF16).reshape(rows, units)
    grad_probs = jnp.sum(hits * dots[:, None, :], axis=2)
    return (output, grad_hidden, grad_weight, grad_probs)


NT = (((1,), (1,)), ((), ()))
NN = (((1,), (0,)), ((), ()))
TN = (((0,), (0,)), ((), ()))


def dot(a, b, dims):
    return lax.dot_general(a, b, dims, preferred_element_type=F32)


def fused_kernel(
    g_ref, hid_ref, rt_ref, pr_ref, w_ref,
    fin_ref, tok_ref, gw_ref, owns_ref, dots_ref,
    hin, htok, tp, wst, wall, hall, gz, gall, gmate, op, oz, oz2, os2, osum, orow, ofin, bp, rx, ry, sx, sy,
    r2x, r2y, dt, dmine, dz,
    wsem, hsem, gsem,
    wss, wsr, hxs, hxr, hys, hyr, h2s, h2r, hms, hmr, g1s, g1r, g2s, g2r, g3s, g3r, gms, gmr,
    ozs, ozr, o2s, o2r, oas, oar, obs, obr, bxs, bxr, bys, byr, cxs, cxr, cys, cyr, ds_, dr_,
):
    p, z = lax.axis_index("fsdp"), lax.axis_index("ep")
    k, c = lax.rem(p, 2), lax.div(p, 2)
    x, y = lax.rem(c, 2), lax.div(c, 2)
    lo, hi = lax.rem(z, 2), lax.div(z, 2)
    xn, yn = c + 1 - 2 * x, c + 2 - 4 * y
    dg = yn + 1 - 2 * x
    z1, z2 = z + 1 - 2 * lo, z + 2 - 4 * hi
    z3 = z2 + 1 - 2 * lo
    zs = (z, z1, z2, z3)
    chips = (c, xn, yn, dg)
    width = gmate.shape[3]
    half = hall.shape[4] // 2
    sub = gz.shape[1]
    tokens = 4 * sub
    mate = (c * 2 + 1 - k, z)
    to_x, to_y, to_d = (xn * 2 + k, z), (yn * 2 + k, z), (dg * 2 + k, z)
    to_z = (None, (p, z1), (p, z2), (p, z3))
    mine = pl.multiple_of(k * width, 128)
    other = pl.multiple_of((1 - k) * width, 128)
    halves = (pl.ds(0, half), pl.ds(half, half))
    sends = []

    def put(src, dst, ssem, rsem, to):
        copy = remote(src, dst, ssem, rsem, to)
        copy.start()
        sends.append(copy)

    def got(dst, ssem, rsem):
        remote(dst, dst, ssem, rsem, mate).wait_recv()

    barrier = pltpu.get_barrier_semaphore()
    partners = [mate, to_x, to_y, to_d, to_z[1], to_z[2], to_z[3]]
    partners += [(q * 2 + 1 - k, z) for q in (xn, yn, dg)]
    for to in partners:
        pl.semaphore_signal(barrier, inc=1, device_id=to, device_id_type=MESH)

    load_h = pltpu.make_async_copy(hid_ref, hin, hsem)
    load_h.start()
    keep = pltpu.make_async_copy(g_ref.at[pl.ds(z * sub, sub)], gz.at[z], gsem)
    keep.start()
    n_w = wsem.shape[0]
    rows_w = width // n_w
    loads = []
    for i in range(n_w):
        rows = pl.ds(i * rows_w, rows_w)
        copy = pltpu.make_async_copy(w_ref.at[rows], wst.at[rows], wsem.at[i])
        copy.start()
        loads.append(copy)

    row = lax.broadcasted_iota(jnp.int32, (tokens, tokens), 0)
    col = lax.broadcasted_iota(jnp.int32, (tokens, tokens), 1)
    earlier = (row < col).astype(BF16)
    for e in range(2):
        hits = rt_ref[...] == e
        named = jnp.sum(hits.astype(F32), axis=0, keepdims=True)
        rank = dot(jnp.broadcast_to(named, (16, tokens)).astype(BF16), earlier, NN)[0:1]
        owns_ref[e] = ((rank == row.astype(F32)) & (named > 0.0)).astype(BF16)
        prob = jnp.sum(jnp.where(hits, pr_ref[...], 0.0), axis=0, keepdims=True)
        tp[e] = jnp.broadcast_to(prob, (tokens, tokens)).T

    pl.semaphore_wait(barrier, len(partners))

    for s in (1, 2, 3):
        put(g_ref.at[pl.ds(zs[s] * sub, sub)], gz.at[z], g1s.at[s], g1r.at[s], to_z[s])
    load_h.wait()
    for e in range(2):
        picked = dot(owns_ref[e], hin[pl.ds(e * tokens, tokens)], TN)
        htok[e] = picked.astype(BF16)
        hall[e, k, c] = (tp[e, :, 0:1] * picked).astype(BF16)
        put(hall.at[e, k, c, :, halves[0]], hall.at[e, k, c, :, halves[0]], hxs.at[e], hxr.at[e], to_x)
        put(hall.at[e, k, c, :, halves[1]], hall.at[e, k, c, :, halves[1]], hys.at[e], hyr.at[e], to_y)
    put(hall.at[:, k, c], hall.at[:, k, c], hms.at[0], hmr.at[0], mate)

    r = lax.broadcasted_iota(jnp.int32, (rows_w, 2 * rows_w), 0)
    q = lax.broadcasted_iota(jnp.int32, (rows_w, 2 * rows_w), 1)
    picks = [(q == 2 * r + e).astype(BF16) for e in range(2)]
    for i in range(n_w):
        loads[i].wait()
        block = wst[pl.ds(i * rows_w, rows_w)].reshape(2 * rows_w, 2 * half)
        rows = pl.ds(mine + i * rows_w, rows_w)
        for e in range(2):
            wall[e, rows] = dot(picks[e], block, NN).astype(BF16)
        put(wall.at[:, rows], wall.at[:, rows], wss.at[i], wsr.at[i], mate)

    def product(g):
        ci = chips[g]
        acc = jnp.zeros((2 * 4 * sub, width), F32)
        for e in range(2):
            acc += dot(hall[e, :, ci].reshape(2 * 4 * sub, 2 * half), wall[e, pl.ds(mine, width)], NT)
        op[g] = acc.astype(BF16).reshape(2, 2, 2, sub, width)
        put(op.at[g, :, :, 1 - lo], oz.at[g], ozs.at[g], ozr.at[g], to_z[1])

    def relay(g):
        got(oz.at[g], ozs.at[g], ozr.at[g])
        os2[g] = (op[g, :, 1 - hi, lo].astype(F32) + oz[g, :, 1 - hi].astype(F32)).astype(BF16)
        put(os2.at[g], oz2.at[g], o2s.at[g], o2r.at[g], to_z[2])

    def deliver(g):
        got(oz2.at[g], o2s.at[g], o2r.at[g])
        osum[g] = (
            op[g, :, hi, lo].astype(F32) + oz[g, :, hi].astype(F32) + oz2[g].astype(F32)
        ).astype(BF16)
        for b in range(2):
            i = b_core(k, b)
            if g or b:
                put(osum.at[g, i], orow.at[c, k], oas.at[g, b], oar.at[g, b], (chips[g] * 2 + i, z))
        if g == 0:
            orow[c, k] = osum[0, k]

    def final(s):
        return remote(orow.at[zs[s]], ofin.at[z], obs.at[s], obr.at[s], to_z[s])

    def pass_on(g):
        for b in range(2):
            if g or b:
                got(orow.at[chips[g], b_core(k, b)], oas.at[g, b], oar.at[g, b])

        @pl.when(chips[g] == z)
        def _():
            ofin[z] = orow[z]

        for s in (1, 2, 3):

            @pl.when(chips[g] == zs[s])
            def _():
                final(s).start()

    def back(s):
        lhs = gall[:, zs[s]].reshape(4 * sub, 2 * width)
        for e in range(2):

            def tile(t, _):
                cols = pl.ds(pl.multiple_of(t * half, 128), half)
                acc = dot(lhs, wall[e, :, cols], NN)
                bp[s, e, :, :, :, cols] = acc.astype(BF16).reshape(2, 2, sub, half)
                return 0

            lax.fori_loop(0, 2, tile, 0)

    def spread_back(s):
        put(bp.at[s, :, :, 1 - x, :, halves[0]], rx.at[s], bxs.at[s], bxr.at[s], to_x)
        put(bp.at[s, :, 1 - y, :, :, halves[1]], ry.at[s], bys.at[s], byr.at[s], to_y)

    def turn(s):
        got(rx.at[s], bxs.at[s], bxr.at[s])
        sy[s] = (bp[s, :, 1 - y, x, :, halves[0]].astype(F32) + rx[s, :, 1 - y].astype(F32)).astype(BF16)
        put(sy.at[s], r2y.at[s], cys.at[s], cyr.at[s], to_y)
        got(ry.at[s], bys.at[s], byr.at[s])
        sx[s] = (bp[s, :, y, 1 - x, :, halves[1]].astype(F32) + ry[s, :, 1 - x].astype(F32)).astype(BF16)
        put(sx.at[s], r2x.at[s], cxs.at[s], cxr.at[s], to_x)

    def settle(s):
        got(r2y.at[s], cys.at[s], cyr.at[s])
        got(r2x.at[s], cxs.at[s], cxr.at[s])
        rows = pl.ds(pl.multiple_of(zs[s] * sub, sub), sub)
        for e in range(2):
            total = jnp.zeros((sub, 1), F32)
            for b in range(2):
                if b == 0:
                    value = rx[s, e, y].astype(F32) + r2y[s, e].astype(F32)
                else:
                    value = ry[s, e, x].astype(F32) + r2x[s, e].astype(F32)
                value += bp[s, e, y, x, :, halves[b]].astype(F32)
                tok_ref[e, rows, halves[b]] = (tp[e, rows, 0:1] * value).astype(BF16)
                total += jnp.sum(htok[e, rows, halves[b]].astype(F32) * value, axis=1, keepdims=True)
            dt[e, rows] = jnp.broadcast_to(total, (sub, 128))

    rows_g = width // 3

    def weight(i):
        rows = pl.ds(i * rows_g, rows_g)
        for e in range(2):

            def tile(t, _):
                cols = pl.ds(pl.multiple_of(t * half, 128), half)
                acc = dot(
                    gall[:, :, :, pl.ds(pl.multiple_of(mine + i * rows_g, 128), rows_g)].reshape(16 * sub, rows_g),
                    hall[e, k, :, :, cols].reshape(16 * sub, half),
                    TN,
                )
                acc += dot(
                    gmate[:, :, :, rows].reshape(16 * sub, rows_g),
                    hall[e, 1 - k, :, :, cols].reshape(16 * sub, half),
                    TN,
                )
                gw_ref[rows, e, cols] = acc.astype(BF16)
                return 0

            lax.fori_loop(0, 2, tile, 0)

    def share(s):
        j = zs[s]
        put(gall.at[:, j, :, pl.ds(other, width)], gmate.at[:, j], gms.at[s], gmr.at[s], mate)

    def own_half(i):
        for e in range(2):
            block = hall.at[e, k, c, :, halves[1 - i]]
            if i == 0:
                put(block, block, hxs.at[2 + e], hxr.at[2 + e], to_x)
            else:
                put(block, block, hys.at[2 + e], hyr.at[2 + e], to_y)

    for s in (1, 2, 3):
        got(gz.at[zs[s]], g1s.at[s], g1r.at[s])
    keep.wait()
    for i, to in ((1, to_x), (2, to_y), (3, to_d)):
        put(gz.at[chips[i]], gall.at[c, z], g2s.at[i], g2r.at[i], to)
    gall[c, z] = gz[c]
    got(hall.at[:, 1 - k, c], hms.at[0], hmr.at[0])
    product(0)
    for i in (1, 2, 3):
        got(gall.at[chips[i], z], g2s.at[i], g2r.at[i])
    put(gall.at[:, z], gall.at[:, z], g3s.at[2], g3r.at[2], to_z[2])
    put(gall.at[:, z], gall.at[:, z], g3s.at[1], g3r.at[1], to_z[1])
    own_half(0)
    own_half(1)
    for e in range(2):
        block = hall.at[e, k, xn, :, halves[0]]
        got(block, hxs.at[e], hxr.at[e])
        put(block, block, h2s.at[e], h2r.at[e], to_y)
        block = hall.at[e, k, yn, :, halves[1]]
        got(block, hys.at[e], hyr.at[e])
        put(block, block, h2s.at[2 + e], h2r.at[2 + e], to_x)
    share(0)
    relay(0)
    for i in range(n_w):
        rows = pl.ds(other + i * rows_w, rows_w)
        got(wall.at[:, rows], wss.at[i], wsr.at[i])
    back(0)
    deliver(0)
    for e in range(2):
        got(hall.at[e, k, xn, :, halves[1]], hxs.at[2 + e], hxr.at[2 + e])
    put(hall.at[:, k, xn], hall.at[:, k, xn], hms.at[1], hmr.at[1], mate)
    for e in range(2):
        got(hall.at[e, k, yn, :, halves[0]], hys.at[2 + e], hyr.at[2 + e])
    put(hall.at[:, k, yn], hall.at[:, k, yn], hms.at[2], hmr.at[2], mate)
    spread_back(0)
    got(hall.at[:, 1 - k, xn], hms.at[1], hmr.at[1])
    product(1)
    got(hall.at[:, 1 - k, yn], hms.at[2], hmr.at[2])
    product(2)
    got(gall.at[:, z2], g3s.at[2], g3r.at[2])
    put(gall.at[:, z2], gall.at[:, z2], g3s.at[3], g3r.at[3], to_z[1])
    share(2)
    back(2)
    spread_back(2)
    for e in range(2):
        got(hall.at[e, k, dg, :, halves[0]], h2s.at[e], h2r.at[e])
        got(hall.at[e, k, dg, :, halves[1]], h2s.at[2 + e], h2r.at[2 + e])
    put(hall.at[:, k, dg], hall.at[:, k, dg], hms.at[3], hmr.at[3], mate)
    relay(1)
    got(hall.at[:, 1 - k, dg], hms.at[3], hmr.at[3])
    product(3)
    relay(2)
    got(gall.at[:, z1], g3s.at[1], g3r.at[1])
    share(1)
    back(1)
    spread_back(1)
    turn(0)
    got(gall.at[:, z3], g3s.at[3], g3r.at[3])
    share(3)
    back(3)
    spread_back(3)
    relay(3)
    deliver(1)
    pass_on(0)
    for s in range(4):
        got(gmate.at[:, zs[s]], gms.at[s], gmr.at[s])
    weight(0)
    turn(2)
    deliver(2)
    pass_on(1)
    deliver(3)
    weight(1)
    turn(1)
    pass_on(2)
    settle(0)
    pass_on(3)
    weight(2)
    turn(3)
    settle(2)
    settle(1)
    for s in (1, 2, 3):
        got(ofin.at[zs[s]], obs.at[s], obr.at[s])
    fin_ref[...] = ofin[...]
    settle(3)
    lane = lax.broadcasted_iota(jnp.int32, (tokens, 128), 1)
    both = jnp.where(lane == 0, dt[0], jnp.where(lane == 1, dt[1], 0.0))
    dmine[...] = both.T[0:8]
    for s in (1, 2, 3):
        put(dmine, dz.at[s], ds_.at[s], dr_.at[s], to_z[s])
    total = dmine[...]
    for s in (1, 2, 3):
        got(dz.at[s], ds_.at[s], dr_.at[s])
        total = total + dz[s]
    dots_ref[...] = total
    for copy in sends:
        copy.wait_send()
    for s in (1, 2, 3):
        final(s).wait_send()


def finish_kernel(gw_in, fin_in, tok_in, owns_ref, dots_ref, rt_ref, gw_ref, out_ref, gh_ref, gp_ref, gh, sem):
    copies = []

    def store(src, dst):
        copies.append(pltpu.make_async_copy(src, dst, sem.at[len(copies)]))
        copies[-1].start()

    rows_n = gw_in.shape[0] // FINISH_PARTS
    for i in range(FINISH_PARTS):
        rows = pl.ds(i * rows_n, rows_n)
        store(gw_in.at[rows], gw_ref.at[rows])
    n_sub, n_half, sub, width = fin_in.shape
    for b in range(n_half):
        for j in range(n_sub):
            store(fin_in.at[j, b], out_ref.at[pl.ds(j * sub, sub), pl.ds(b * width, width)])
    total = jnp.zeros(gp_ref.shape, F32)
    for e in range(2):
        total += jnp.where(rt_ref[...] == e, dots_ref[e : e + 1], 0.0)
    gp_ref[...] = total
    for e in range(2):
        gh[e] = dot(owns_ref[e], tok_in[e], NN).astype(BF16)
        store(gh.at[e], gh_ref.at[e])
    for copy in copies:
        copy.wait()


def b_core(k, b):
    return 1 - k if b else k


def fused(grad_out, hidden, routes, probs, w_down):
    tokens = grad_out.shape[0]
    width, _, units = w_down.shape
    sub = tokens // 4
    half = units // 2
    dma = pltpu.SemaphoreType.DMA
    vmem = lambda *shape: pltpu.VMEM(shape, BF16)
    anywhere = pl.BlockSpec(memory_space=pl.ANY)
    scratch = [
        vmem(2 * tokens, units),
        vmem(2, tokens, units),
        pltpu.VMEM((2, tokens, tokens), F32),
        vmem(width, 2, units),
        vmem(2, 2 * width, units),
        vmem(2, 2, 4, tokens, units),
        vmem(4, sub, 2 * width),
        vmem(4, 4, sub, 2 * width),
        vmem(4, 4, sub, width),
        vmem(4, 2, 2, 2, sub, width),
        vmem(4, 2, 2, sub, width),
        vmem(4, 2, sub, width),
        vmem(4, 2, sub, width),
        vmem(4, 2, sub, width),
        vmem(4, 2, sub, width),
        vmem(4, 2, sub, width),
        vmem(4, 2, 2, 2, sub, units),
        vmem(4, 2, 2, sub, half),
        vmem(4, 2, 2, sub, half),
        vmem(4, 2, sub, half),
        vmem(4, 2, sub, half),
        vmem(4, 2, sub, half),
        vmem(4, 2, sub, half),
        pltpu.VMEM((2, tokens, 128), F32),
        pltpu.VMEM((8, 128), F32),
        pltpu.VMEM((4, 8, 128), F32),
        dma((6,)),
        dma,
        dma,
    ]
    for n in ((6,),) + ((4,),) * 10 + ((4, 2),) + ((4,),) * 6:
        scratch += [dma(n), dma(n)]
    fin, tok, weight, owns, dots = pl.pallas_call(
        fused_kernel,
        out_shape=(
            vmem(4, 2, sub, width),
            vmem(2, tokens, units),
            vmem(width, 2, units),
            vmem(2, tokens, tokens),
            pltpu.VMEM((8, 128), F32),
        ),
        in_specs=[anywhere, anywhere, VMEM, VMEM, anywhere],
        out_specs=(VMEM, VMEM, VMEM, VMEM, VMEM),
        scratch_shapes=scratch,
        compiler_params=pltpu.CompilerParams(
            collective_id=3, has_side_effects=True, vmem_limit_bytes=VMEM_LIMIT
        ),
    )(grad_out, hidden, routes, probs, w_down)
    return pl.pallas_call(
        finish_kernel,
        out_shape=(
            jax.ShapeDtypeStruct((width, 2, units), BF16),
            jax.ShapeDtypeStruct((tokens, 2 * width), BF16),
            jax.ShapeDtypeStruct((2, tokens, units), BF16),
            jax.ShapeDtypeStruct((2, tokens), F32),
        ),
        in_specs=[VMEM] * 6,
        out_specs=(anywhere, anywhere, anywhere, VMEM),
        scratch_shapes=[vmem(2, tokens, units), dma((FINISH_PARTS + 10,))],
        compiler_params=pltpu.CompilerParams(vmem_limit_bytes=16 * 2**20),
    )(weight, fin, tok, owns, dots, routes)


def local_fused(hidden, w_down, route_ids, probs, grad_out):
    grad_weight, output, grad_hidden, grad_probs = fused(
        grad_out, hidden, route_ids.T, probs.T, w_down
    )
    return (output, grad_hidden.reshape(hidden.shape), grad_weight, grad_probs.T)


def solution(mesh):
    placed = (
        P("fsdp", "ep"),
        P("fsdp", None, "ep"),
        P("fsdp", None),
        P("fsdp", None),
        P("fsdp", "ep"),
    )
    n_fsdp, n_ep = mesh.shape["fsdp"], mesh.shape["ep"]
    if (n_fsdp, n_ep) == (8, 4):
        body = local_fused
    else:
        body = functools.partial(local, n_fsdp, n_ep)
    return jax.shard_map(
        body,
        mesh=mesh,
        in_specs=placed,
        out_specs=(P("fsdp", "ep"), P("fsdp", "ep"), P("fsdp", None, "ep"), P("fsdp", None)),
        check_vma=False,
    )
```

```python
import functools

import jax
import jax.numpy as jnp
from jax import lax
from jax.experimental import pallas as pl
from jax.experimental.layout import Layout, with_layout_constraint
from jax.experimental.pallas import tpu as pltpu
from jax.sharding import PartitionSpec as P

F32 = jnp.float32
BF16 = jnp.bfloat16
MESH = pl.DeviceIdType.MESH
VMEM = pl.BlockSpec(memory_space=pltpu.VMEM)
VMEM_LIMIT = 50 * 2**20
FINISH_PARTS = 6


def meet(n_fsdp, n_ep, p, z):
    barrier = pltpu.get_barrier_semaphore()
    for s in range(1, n_ep):
        pl.semaphore_signal(
            barrier, inc=1, device_id=(p, lax.rem(z + s, n_ep)), device_id_type=MESH
        )
    for s in range(1, n_fsdp):
        pl.semaphore_signal(
            barrier, inc=1, device_id=(lax.rem(p + s, n_fsdp), z), device_id_type=MESH
        )
    pl.semaphore_wait(barrier, n_ep - 1 + n_fsdp - 1)


def remote(src, dst, send, recv, to):
    return pltpu.make_async_remote_copy(
        src_ref=src, dst_ref=dst, send_sem=send, recv_sem=recv, device_id=to, device_id_type=MESH
    )


def spread_kernel(
    n_fsdp, n_ep, g_ref, h_ref, out_ref, hall_ref, held, zsend, zrecv, psend, precv, hsend, fsend, hrecv, own
):
    ratio = g_ref.shape[0]
    n_chip = n_fsdp // 2
    p, z = lax.axis_index("fsdp"), lax.axis_index("ep")
    chip, core = lax.div(p, 2), lax.rem(p, 2)
    mate = chip * 2 + 1 - core
    meet(n_fsdp, n_ep, p, z)
    sends = []
    for s in range(1, n_ep):
        copy = remote(g_ref, held.at[z], zsend.at[s], zrecv.at[z], (p, lax.rem(z + s, n_ep)))
        copy.start()
        sends.append(copy)
    keep = pltpu.make_async_copy(h_ref, hall_ref.at[:, p], own)
    keep.start()

    def pieces(s, act):
        q = lax.rem(z + n_ep - s, n_ep)
        for r in range(ratio):
            block = held.at[q, r] if s else g_ref.at[r]
            i = q * ratio + r

            @pl.when(i != p)
            def _():
                act(remote(block, out_ref.at[p], psend.at[s, r], precv.at[p], (i, z)))

            if act is begin:

                @pl.when(i == p)
                def _():
                    out_ref[p] = block[...]

    def begin(copy):
        copy.start()

    def end(copy):
        copy.wait_send()

    pieces(0, begin)
    for s in range(1, n_chip):
        to = lax.rem(chip + s, n_chip) * 2 + core
        copy = remote(h_ref, hall_ref.at[:, p], hsend.at[s], hrecv.at[p], (to, z))
        copy.start()
        sends.append(copy)
    copy = remote(h_ref, hall_ref.at[:, p], hsend.at[0], hrecv.at[p], (mate, z))
    copy.start()
    sends.append(copy)
    for s in range(1, max(n_ep, n_chip)):
        if s < n_ep:
            q = lax.rem(z + n_ep - s, n_ep)
            remote(g_ref, held.at[q], zsend.at[s], zrecv.at[q], (p, z)).wait_recv()
            pieces(s, begin)
        if s < n_chip:
            f = lax.rem(chip + n_chip - s, n_chip) * 2 + core
            copy = remote(hall_ref.at[:, f], hall_ref.at[:, f], fsend.at[s], hrecv.at[f], (mate, z))
            copy.wait_recv()
            copy.start()
            sends.append(copy)
    for s in range(n_chip):
        f = lax.rem(chip + s, n_chip) * 2 + 1 - core
        remote(h_ref, hall_ref.at[:, f], hsend.at[0], hrecv.at[f], (mate, z)).wait_recv()
    for s in range(1, n_fsdp):
        f = lax.rem(p + s, n_fsdp)
        remote(g_ref.at[0], out_ref.at[f], psend.at[0, 0], precv.at[f], (f, z)).wait_recv()
    for s in range(n_ep):
        pieces(s, end)
    for copy in sends:
        copy.wait_send()
    keep.wait()


def collect_kernel(n_fsdp, n_ep, part_ref, out_ref, held, sums, psend, precv, zsend, zrecv):
    ratio = out_ref.shape[0]
    p, z = lax.axis_index("fsdp"), lax.axis_index("ep")
    meet(n_fsdp, n_ep, p, z)
    held[p] = part_ref[p]
    across = []
    for s in range(1, n_fsdp):
        i = lax.rem(p + s, n_fsdp)
        copy = remote(part_ref.at[i], held.at[p], psend.at[s], precv.at[p], (i, z))
        copy.start()
        across.append(copy)
    along = []
    for s in range(1, n_ep + 1):
        q = lax.rem(z + s, n_ep)
        for r in range(ratio):
            f = q * ratio + r

            @pl.when(f != p)
            def _():
                remote(part_ref.at[0], held.at[f], psend.at[0], precv.at[f], (p, z)).wait_recv()

        if s < n_ep:
            copy = remote(
                held.at[pl.ds(q * ratio, ratio)], sums.at[z], zsend.at[s], zrecv.at[z], (p, q)
            )
            copy.start()
            along.append(copy)
    total = held[pl.ds(z * ratio, ratio)].astype(F32)
    for s in range(1, n_ep):
        q = lax.rem(z + s, n_ep)
        remote(
            held.at[pl.ds(q * ratio, ratio)], sums.at[q], zsend.at[s], zrecv.at[q], (p, q)
        ).wait_recv()
        total = total + sums[q].astype(F32)
    out_ref[...] = total.astype(BF16)
    for copy in across + along:
        copy.wait_send()


def add_kernel(n_ep, x_ref, out_ref, held, send, recv):
    p, z = lax.axis_index("fsdp"), lax.axis_index("ep")
    meet(1, n_ep, p, z)
    copies = []
    for s in range(1, n_ep):
        copy = remote(x_ref, held.at[z], send.at[s], recv.at[z], (p, lax.rem(z + s, n_ep)))
        copy.start()
        copies.append(copy)
    total = x_ref[...]
    for s in range(1, n_ep):
        q = lax.rem(z + s, n_ep)
        remote(x_ref, held.at[q], send.at[s], recv.at[q], (p, q)).wait_recv()
        total = total + held[q]
    out_ref[...] = total
    for copy in copies:
        copy.wait_send()


def talk(body, key, x, shape, scratch, flops=0):
    return pl.pallas_call(
        body,
        out_shape=jax.ShapeDtypeStruct(shape, x.dtype),
        in_specs=[VMEM],
        out_specs=VMEM,
        scratch_shapes=scratch,
        cost_estimate=pl.CostEstimate(flops=flops, bytes_accessed=100_000_000, transcendentals=0),
        compiler_params=pltpu.CompilerParams(collective_id=key, has_side_effects=True),
    )(x)


def spread(grad_out, scaled, n_fsdp, n_ep):
    tokens, width = grad_out.shape
    experts, _, units = scaled.shape
    ratio = n_fsdp // n_ep
    cut = width // ratio
    blocks = jnp.stack([grad_out[:, r * cut : (r + 1) * cut] for r in range(ratio)])
    dma = pltpu.SemaphoreType.DMA
    anywhere = pl.BlockSpec(memory_space=pl.ANY)
    out, hid_all = pl.pallas_call(
        functools.partial(spread_kernel, n_fsdp, n_ep),
        out_shape=(
            jax.ShapeDtypeStruct((n_fsdp, tokens, cut), BF16),
            jax.ShapeDtypeStruct((experts, n_fsdp, tokens, units), BF16),
        ),
        in_specs=[VMEM, anywhere],
        out_specs=(VMEM, anywhere),
        scratch_shapes=[
            pltpu.VMEM((n_ep, ratio, tokens, cut), BF16),
            dma((n_ep,)),
            dma((n_ep,)),
            dma((n_ep, ratio)),
            dma((n_fsdp,)),
            dma((n_fsdp // 2,)),
            dma((n_fsdp // 2,)),
            dma((n_fsdp,)),
            dma,
        ],
        compiler_params=pltpu.CompilerParams(collective_id=0, has_side_effects=True),
    )(blocks, scaled)
    return out.reshape(n_fsdp * tokens, cut), hid_all.reshape(experts, n_fsdp * tokens, units)


def collect(part, n_fsdp, n_ep):
    cut = part.shape[1]
    tokens = part.shape[0] // n_fsdp
    ratio = n_fsdp // n_ep
    dma = pltpu.SemaphoreType.DMA
    out = talk(
        functools.partial(collect_kernel, n_fsdp, n_ep),
        1,
        part.reshape(n_fsdp, tokens, cut),
        (ratio, tokens, cut),
        [
            pltpu.VMEM((n_fsdp, tokens, cut), BF16),
            pltpu.VMEM((n_ep, ratio, tokens, cut), BF16),
            dma((n_fsdp,)),
            dma((n_fsdp,)),
            dma((n_ep,)),
            dma((n_ep,)),
        ],
    )
    return jnp.concatenate([out[r] for r in range(ratio)], axis=1)


def add_up(x, n_ep):
    dma = pltpu.SemaphoreType.DMA
    return talk(
        functools.partial(add_kernel, n_ep),
        2,
        x,
        x.shape,
        [pltpu.VMEM((n_ep,) + x.shape, F32), dma((n_ep,)), dma((n_ep,))],
    )


def route_maps(route_ids, probs, experts):
    tokens = route_ids.shape[0]
    names = jnp.arange(experts, dtype=jnp.int32)
    hits = (route_ids[:, :, None] == names[None, None, :]).astype(F32)
    named = jnp.sum(hits, axis=1)
    place = jnp.arange(tokens, dtype=jnp.int32)
    earlier = (place[None, :] < place[:, None]).astype(F32)
    rank = jnp.sum(earlier[:, :, None] * named[None, :, :], axis=1).astype(jnp.int32)
    token_prob = jnp.sum(hits * probs[:, :, None], axis=1)
    owns = (rank.T[:, :, None] == place[None, None, :]) & (named.T[:, :, None] > 0)
    return hits, token_prob, owns.astype(BF16)


def local(n_fsdp, n_ep, hidden, w_down, route_ids, probs, grad_out):
    rows, units = hidden.shape
    experts = w_down.shape[1]
    tokens = route_ids.shape[0]
    hits, token_prob, owns = route_maps(route_ids, probs, experts)
    hid_tok = jnp.einsum(
        "etr,erf->etf", owns, hidden.reshape(experts, tokens, units), preferred_element_type=F32
    )
    scaled = (token_prob.T[:, :, None] * hid_tok).astype(BF16)
    hid_tok = hid_tok.astype(BF16)
    grads, hid_all = spread(grad_out, scaled, n_fsdp, n_ep)
    back_part = jnp.einsum("td,def->tef", grads, w_down, preferred_element_type=F32).astype(BF16)
    hid_all, back_part = lax.optimization_barrier((hid_all, back_part))
    back = lax.psum_scatter(back_part, "fsdp", scatter_dimension=0, tiled=True)
    part = jnp.einsum("etf,def->td", hid_all, w_down, preferred_element_type=F32).astype(BF16)
    output = collect(part, n_fsdp, n_ep)
    grad_weight = jnp.einsum("td,etf->def", grads, hid_all, preferred_element_type=F32).astype(BF16)
    grad_weight = with_layout_constraint(grad_weight, Layout(major_to_minor=(0, 1, 2)))
    back, output, grad_weight = lax.optimization_barrier((back, output, grad_weight))
    back = back.astype(F32)
    dots = jnp.sum(hid_tok.transpose(1, 0, 2).astype(F32) * back, axis=2)
    dots = add_up(dots.T, n_ep).T
    grad_tok = (token_prob[:, :, None] * back).astype(BF16)
    grad_hidden = jnp.einsum("etr,tef->erf", owns, grad_tok, preferred_element_type=F32)
    grad_hidden = grad_hidden.astype(BF16).reshape(rows, units)
    grad_probs = jnp.sum(hits * dots[:, None, :], axis=2)
    return (output, grad_hidden, grad_weight, grad_probs)


NT = (((1,), (1,)), ((), ()))
NN = (((1,), (0,)), ((), ()))
TN = (((0,), (0,)), ((), ()))


def dot(a, b, dims):
    return lax.dot_general(a, b, dims, preferred_element_type=F32)


def fused_kernel(
    g_ref, hid_ref, rt_ref, pr_ref, w_ref,
    fin_ref, tok_ref, gw_ref, owns_ref, dots_ref,
    hin, htok, tp, wst, wall, hall, gz, gall, gmate, op, oz, oz2, os2, osum, orow, ofin, bp, rx, ry, sx, sy,
    r2x, r2y, dt, dmine, dz,
    wsem, hsem, gsem,
    wss, wsr, hxs, hxr, hys, hyr, h2s, h2r, hms, hmr, g1s, g1r, g2s, g2r, g3s, g3r, gms, gmr,
    ozs, ozr, o2s, o2r, oas, oar, obs, obr, bxs, bxr, bys, byr, cxs, cxr, cys, cyr, ds_, dr_,
):
    p, z = lax.axis_index("fsdp"), lax.axis_index("ep")
    k, c = lax.rem(p, 2), lax.div(p, 2)
    x, y = lax.rem(c, 2), lax.div(c, 2)
    lo, hi = lax.rem(z, 2), lax.div(z, 2)
    xn, yn = c + 1 - 2 * x, c + 2 - 4 * y
    dg = yn + 1 - 2 * x
    z1, z2 = z + 1 - 2 * lo, z + 2 - 4 * hi
    z3 = z2 + 1 - 2 * lo
    zs = (z, z1, z2, z3)
    chips = (c, xn, yn, dg)
    width = gmate.shape[3]
    half = hall.shape[4] // 2
    sub = gz.shape[1]
    tokens = 4 * sub
    mate = (c * 2 + 1 - k, z)
    to_x, to_y, to_d = (xn * 2 + k, z), (yn * 2 + k, z), (dg * 2 + k, z)
    to_z = (None, (p, z1), (p, z2), (p, z3))
    mine = pl.multiple_of(k * width, 128)
    other = pl.multiple_of((1 - k) * width, 128)
    halves = (pl.ds(0, half), pl.ds(half, half))
    sends = []

    def put(src, dst, ssem, rsem, to):
        copy = remote(src, dst, ssem, rsem, to)
        copy.start()
        sends.append(copy)

    def got(dst, ssem, rsem):
        remote(dst, dst, ssem, rsem, mate).wait_recv()

    barrier = pltpu.get_barrier_semaphore()
    partners = [mate, to_x, to_y, to_d, to_z[1], to_z[2], to_z[3]]
    partners += [(q * 2 + 1 - k, z) for q in (xn, yn, dg)]
    for to in partners:
        pl.semaphore_signal(barrier, inc=1, device_id=to, device_id_type=MESH)

    load_h = pltpu.make_async_copy(hid_ref, hin, hsem)
    load_h.start()
    keep = pltpu.make_async_copy(g_ref.at[pl.ds(z * sub, sub)], gz.at[z], gsem)
    keep.start()
    n_w = wsem.shape[0]
    rows_w = width // n_w
    loads = []
    for i in range(n_w):
        rows = pl.ds(i * rows_w, rows_w)
        copy = pltpu.make_async_copy(w_ref.at[rows], wst.at[rows], wsem.at[i])
        copy.start()
        loads.append(copy)

    row = lax.broadcasted_iota(jnp.int32, (tokens, tokens), 0)
    col = lax.broadcasted_iota(jnp.int32, (tokens, tokens), 1)
    earlier = (row < col).astype(BF16)
    for e in range(2):
        hits = rt_ref[...] == e
        named = jnp.sum(hits.astype(F32), axis=0, keepdims=True)
        rank = dot(jnp.broadcast_to(named, (16, tokens)).astype(BF16), earlier, NN)[0:1]
        owns_ref[e] = ((rank == row.astype(F32)) & (named > 0.0)).astype(BF16)
        prob = jnp.sum(jnp.where(hits, pr_ref[...], 0.0), axis=0, keepdims=True)
        tp[e] = jnp.broadcast_to(prob, (tokens, tokens)).T

    pl.semaphore_wait(barrier, len(partners))

    for s in (1, 2, 3):
        put(g_ref.at[pl.ds(zs[s] * sub, sub)], gz.at[z], g1s.at[s], g1r.at[s], to_z[s])
    load_h.wait()
    for e in range(2):
        picked = dot(owns_ref[e], hin[pl.ds(e * tokens, tokens)], TN)
        htok[e] = picked.astype(BF16)
        hall[e, k, c] = (tp[e, :, 0:1] * picked).astype(BF16)
        if e == 0:
            put(hall.at[e, k, c, :, halves[0]], hall.at[e, k, c, :, halves[0]], hxs.at[e], hxr.at[e], to_x)
            put(hall.at[e, k, c, :, halves[1]], hall.at[e, k, c, :, halves[1]], hys.at[e], hyr.at[e], to_y)
    put(hall.at[:, k, c], hall.at[:, k, c], hms.at[0], hmr.at[0], mate)

    r = lax.broadcasted_iota(jnp.int32, (rows_w, 2 * rows_w), 0)
    q = lax.broadcasted_iota(jnp.int32, (rows_w, 2 * rows_w), 1)
    picks = [(q == 2 * r + e).astype(BF16) for e in range(2)]
    for i in range(n_w):
        loads[i].wait()
        block = wst[pl.ds(i * rows_w, rows_w)].reshape(2 * rows_w, 2 * half)
        rows = pl.ds(mine + i * rows_w, rows_w)
        for e in range(2):
            wall[e, rows] = dot(picks[e], block, NN).astype(BF16)
        put(wall.at[:, rows], wall.at[:, rows], wss.at[i], wsr.at[i], mate)

    def product(g):
        ci = chips[g]
        acc = jnp.zeros((2 * 4 * sub, width), F32)
        for e in range(2):
            acc += dot(hall[e, :, ci].reshape(2 * 4 * sub, 2 * half), wall[e, pl.ds(mine, width)], NT)
        op[g] = acc.astype(BF16).reshape(2, 2, 2, sub, width)
        put(op.at[g, :, :, 1 - lo], oz.at[g], ozs.at[g], ozr.at[g], to_z[1])

    def relay(g):
        got(oz.at[g], ozs.at[g], ozr.at[g])
        os2[g] = (op[g, :, 1 - hi, lo].astype(F32) + oz[g, :, 1 - hi].astype(F32)).astype(BF16)
        put(os2.at[g], oz2.at[g], o2s.at[g], o2r.at[g], to_z[2])

    def deliver(g):
        got(oz2.at[g], o2s.at[g], o2r.at[g])
        osum[g] = (
            op[g, :, hi, lo].astype(F32) + oz[g, :, hi].astype(F32) + oz2[g].astype(F32)
        ).astype(BF16)
        for b in range(2):
            i = b_core(k, b)
            if g or b:
                put(osum.at[g, i], orow.at[c, k], oas.at[g, b], oar.at[g, b], (chips[g] * 2 + i, z))
        if g == 0:
            orow[c, k] = osum[0, k]

    def final(s):
        return remote(orow.at[zs[s]], ofin.at[z], obs.at[s], obr.at[s], to_z[s])

    def pass_on(g):
        for b in range(2):
            if g or b:
                got(orow.at[chips[g], b_core(k, b)], oas.at[g, b], oar.at[g, b])

        @pl.when(chips[g] == z)
        def _():
            ofin[z] = orow[z]

        for s in (1, 2, 3):

            @pl.when(chips[g] == zs[s])
            def _():
                final(s).start()

    def back(s):
        lhs = gall[:, zs[s]].reshape(4 * sub, 2 * width)
        for e in range(2):

            def tile(t, _):
                cols = pl.ds(pl.multiple_of(t * half, 128), half)
                acc = dot(lhs, wall[e, :, cols], NN)
                bp[s, e, :, :, :, cols] = acc.astype(BF16).reshape(2, 2, sub, half)
                return 0

            lax.fori_loop(0, 2, tile, 0)

    def spread_back(s):
        put(bp.at[s, :, :, 1 - x, :, halves[0]], rx.at[s], bxs.at[s], bxr.at[s], to_x)
        put(bp.at[s, :, 1 - y, :, :, halves[1]], ry.at[s], bys.at[s], byr.at[s], to_y)

    def turn(s):
        got(rx.at[s], bxs.at[s], bxr.at[s])
        sy[s] = (bp[s, :, 1 - y, x, :, halves[0]].astype(F32) + rx[s, :, 1 - y].astype(F32)).astype(BF16)
        put(sy.at[s], r2y.at[s], cys.at[s], cyr.at[s], to_y)
        got(ry.at[s], bys.at[s], byr.at[s])
        sx[s] = (bp[s, :, y, 1 - x, :, halves[1]].astype(F32) + ry[s, :, 1 - x].astype(F32)).astype(BF16)
        put(sx.at[s], r2x.at[s], cxs.at[s], cxr.at[s], to_x)

    def settle(s):
        got(r2y.at[s], cys.at[s], cyr.at[s])
        got(r2x.at[s], cxs.at[s], cxr.at[s])
        rows = pl.ds(pl.multiple_of(zs[s] * sub, sub), sub)
        for e in range(2):
            total = jnp.zeros((sub, 1), F32)
            for b in range(2):
                if b == 0:
                    value = rx[s, e, y].astype(F32) + r2y[s, e].astype(F32)
                else:
                    value = ry[s, e, x].astype(F32) + r2x[s, e].astype(F32)
                value += bp[s, e, y, x, :, halves[b]].astype(F32)
                tok_ref[e, rows, halves[b]] = (tp[e, rows, 0:1] * value).astype(BF16)
                total += jnp.sum(htok[e, rows, halves[b]].astype(F32) * value, axis=1, keepdims=True)
            dt[e, rows] = jnp.broadcast_to(total, (sub, 128))

    rows_g = width // 3

    def weight(i):
        rows = pl.ds(i * rows_g, rows_g)
        for e in range(2):

            def tile(t, _):
                cols = pl.ds(pl.multiple_of(t * half, 128), half)
                acc = dot(
                    gall[:, :, :, pl.ds(pl.multiple_of(mine + i * rows_g, 128), rows_g)].reshape(16 * sub, rows_g),
                    hall[e, k, :, :, cols].reshape(16 * sub, half),
                    TN,
                )
                acc += dot(
                    gmate[:, :, :, rows].reshape(16 * sub, rows_g),
                    hall[e, 1 - k, :, :, cols].reshape(16 * sub, half),
                    TN,
                )
                gw_ref[rows, e, cols] = acc.astype(BF16)
                return 0

            lax.fori_loop(0, 2, tile, 0)

    def share(s):
        j = zs[s]
        put(gall.at[:, j, :, pl.ds(other, width)], gmate.at[:, j], gms.at[s], gmr.at[s], mate)

    def own_half(i):
        for e in range(2):
            block = hall.at[e, k, c, :, halves[1 - i]]
            if i == 0:
                put(block, block, hxs.at[2 + e], hxr.at[2 + e], to_x)
            else:
                put(block, block, hys.at[2 + e], hyr.at[2 + e], to_y)

    for s in (1, 2, 3):
        got(gz.at[zs[s]], g1s.at[s], g1r.at[s])
    keep.wait()
    for i, to in ((1, to_x), (2, to_y), (3, to_d)):
        put(gz.at[chips[i]], gall.at[c, z], g2s.at[i], g2r.at[i], to)
    gall[c, z] = gz[c]
    got(hall.at[:, 1 - k, c], hms.at[0], hmr.at[0])
    product(0)
    for i in (1, 2, 3):
        got(gall.at[chips[i], z], g2s.at[i], g2r.at[i])
    put(gall.at[:, z], gall.at[:, z], g3s.at[2], g3r.at[2], to_z[2])
    put(gall.at[:, z], gall.at[:, z], g3s.at[1], g3r.at[1], to_z[1])
    for e in (1,):
        put(hall.at[e, k, c, :, halves[0]], hall.at[e, k, c, :, halves[0]], hxs.at[e], hxr.at[e], to_x)
        put(hall.at[e, k, c, :, halves[1]], hall.at[e, k, c, :, halves[1]], hys.at[e], hyr.at[e], to_y)
    own_half(0)
    own_half(1)
    for e in range(2):
        block = hall.at[e, k, xn, :, halves[0]]
        got(block, hxs.at[e], hxr.at[e])
        put(block, block, h2s.at[e], h2r.at[e], to_y)
        block = hall.at[e, k, yn, :, halves[1]]
        got(block, hys.at[e], hyr.at[e])
        put(block, block, h2s.at[2 + e], h2r.at[2 + e], to_x)
    share(0)
    relay(0)
    for i in range(n_w):
        rows = pl.ds(other + i * rows_w, rows_w)
        got(wall.at[:, rows], wss.at[i], wsr.at[i])
    back(0)
    deliver(0)
    for e in range(2):
        got(hall.at[e, k, xn, :, halves[1]], hxs.at[2 + e], hxr.at[2 + e])
    put(hall.at[:, k, xn], hall.at[:, k, xn], hms.at[1], hmr.at[1], mate)
    for e in range(2):
        got(hall.at[e, k, yn, :, halves[0]], hys.at[2 + e], hyr.at[2 + e])
    put(hall.at[:, k, yn], hall.at[:, k, yn], hms.at[2], hmr.at[2], mate)
    spread_back(0)
    got(hall.at[:, 1 - k, xn], hms.at[1], hmr.at[1])
    product(1)
    got(hall.at[:, 1 - k, yn], hms.at[2], hmr.at[2])
    product(2)
    got(gall.at[:, z2], g3s.at[2], g3r.at[2])
    put(gall.at[:, z2], gall.at[:, z2], g3s.at[3], g3r.at[3], to_z[1])
    share(2)
    back(2)
    spread_back(2)
    for e in range(2):
        got(hall.at[e, k, dg, :, halves[0]], h2s.at[e], h2r.at[e])
        got(hall.at[e, k, dg, :, halves[1]], h2s.at[2 + e], h2r.at[2 + e])
    put(hall.at[:, k, dg], hall.at[:, k, dg], hms.at[3], hmr.at[3], mate)
    relay(1)
    got(hall.at[:, 1 - k, dg], hms.at[3], hmr.at[3])
    product(3)
    relay(2)
    got(gall.at[:, z1], g3s.at[1], g3r.at[1])
    share(1)
    back(1)
    spread_back(1)
    turn(0)
    got(gall.at[:, z3], g3s.at[3], g3r.at[3])
    share(3)
    back(3)
    spread_back(3)
    relay(3)
    deliver(1)
    pass_on(0)
    for s in range(4):
        got(gmate.at[:, zs[s]], gms.at[s], gmr.at[s])
    weight(0)
    turn(2)
    deliver(2)
    pass_on(1)
    deliver(3)
    weight(1)
    turn(1)
    pass_on(2)
    settle(0)
    pass_on(3)
    weight(2)
    turn(3)
    settle(2)
    settle(1)
    for s in (1, 2, 3):
        got(ofin.at[zs[s]], obs.at[s], obr.at[s])
    fin_ref[...] = ofin[...]
    settle(3)
    lane = lax.broadcasted_iota(jnp.int32, (tokens, 128), 1)
    both = jnp.where(lane == 0, dt[0], jnp.where(lane == 1, dt[1], 0.0))
    dmine[...] = both.T[0:8]
    for s in (1, 2, 3):
        put(dmine, dz.at[s], ds_.at[s], dr_.at[s], to_z[s])
    total = dmine[...]
    for s in (1, 2, 3):
        got(dz.at[s], ds_.at[s], dr_.at[s])
        total = total + dz[s]
    dots_ref[...] = total
    for copy in sends:
        copy.wait_send()
    for s in (1, 2, 3):
        final(s).wait_send()


def finish_kernel(gw_in, fin_in, tok_in, owns_ref, dots_ref, rt_ref, gw_ref, out_ref, gh_ref, gp_ref, gh, sem):
    copies = []

    def store(src, dst):
        copies.append(pltpu.make_async_copy(src, dst, sem.at[len(copies)]))
        copies[-1].start()

    rows_n = gw_in.shape[0] // FINISH_PARTS
    for i in range(FINISH_PARTS):
        rows = pl.ds(i * rows_n, rows_n)
        store(gw_in.at[rows], gw_ref.at[rows])
    n_sub, n_half, sub, width = fin_in.shape
    for b in range(n_half):
        for j in range(n_sub):
            store(fin_in.at[j, b], out_ref.at[pl.ds(j * sub, sub), pl.ds(b * width, width)])
    total = jnp.zeros(gp_ref.shape, F32)
    for e in range(2):
        total += jnp.where(rt_ref[...] == e, dots_ref[e : e + 1], 0.0)
    gp_ref[...] = total
    for e in range(2):
        gh[e] = dot(owns_ref[e], tok_in[e], NN).astype(BF16)
        store(gh.at[e], gh_ref.at[e])
    for copy in copies:
        copy.wait()


def b_core(k, b):
    return 1 - k if b else k


def fused(grad_out, hidden, routes, probs, w_down):
    tokens = grad_out.shape[0]
    width, _, units = w_down.shape
    sub = tokens // 4
    half = units // 2
    dma = pltpu.SemaphoreType.DMA
    vmem = lambda *shape: pltpu.VMEM(shape, BF16)
    anywhere = pl.BlockSpec(memory_space=pl.ANY)
    scratch = [
        vmem(2 * tokens, units),
        vmem(2, tokens, units),
        pltpu.VMEM((2, tokens, tokens), F32),
        vmem(width, 2, units),
        vmem(2, 2 * width, units),
        vmem(2, 2, 4, tokens, units),
        vmem(4, sub, 2 * width),
        vmem(4, 4, sub, 2 * width),
        vmem(4, 4, sub, width),
        vmem(4, 2, 2, 2, sub, width),
        vmem(4, 2, 2, sub, width),
        vmem(4, 2, sub, width),
        vmem(4, 2, sub, width),
        vmem(4, 2, sub, width),
        vmem(4, 2, sub, width),
        vmem(4, 2, sub, width),
        vmem(4, 2, 2, 2, sub, units),
        vmem(4, 2, 2, sub, half),
        vmem(4, 2, 2, sub, half),
        vmem(4, 2, sub, half),
        vmem(4, 2, sub, half),
        vmem(4, 2, sub, half),
        vmem(4, 2, sub, half),
        pltpu.VMEM((2, tokens, 128), F32),
        pltpu.VMEM((8, 128), F32),
        pltpu.VMEM((4, 8, 128), F32),
        dma((6,)),
        dma,
        dma,
    ]
    for n in ((6,),) + ((4,),) * 10 + ((4, 2),) + ((4,),) * 6:
        scratch += [dma(n), dma(n)]
    fin, tok, weight, owns, dots = pl.pallas_call(
        fused_kernel,
        out_shape=(
            vmem(4, 2, sub, width),
            vmem(2, tokens, units),
            vmem(width, 2, units),
            vmem(2, tokens, tokens),
            pltpu.VMEM((8, 128), F32),
        ),
        in_specs=[anywhere, anywhere, VMEM, VMEM, anywhere],
        out_specs=(VMEM, VMEM, VMEM, VMEM, VMEM),
        scratch_shapes=scratch,
        compiler_params=pltpu.CompilerParams(
            collective_id=3, has_side_effects=True, vmem_limit_bytes=VMEM_LIMIT
        ),
    )(grad_out, hidden, routes, probs, w_down)
    return pl.pallas_call(
        finish_kernel,
        out_shape=(
            jax.ShapeDtypeStruct((width, 2, units), BF16),
            jax.ShapeDtypeStruct((tokens, 2 * width), BF16),
            jax.ShapeDtypeStruct((2, tokens, units), BF16),
            jax.ShapeDtypeStruct((2, tokens), F32),
        ),
        in_specs=[VMEM] * 6,
        out_specs=(anywhere, anywhere, anywhere, VMEM),
        scratch_shapes=[vmem(2, tokens, units), dma((FINISH_PARTS + 10,))],
        compiler_params=pltpu.CompilerParams(vmem_limit_bytes=16 * 2**20),
    )(weight, fin, tok, owns, dots, routes)


def local_fused(hidden, w_down, route_ids, probs, grad_out):
    grad_weight, output, grad_hidden, grad_probs = fused(
        grad_out, hidden, route_ids.T, probs.T, w_down
    )
    return (output, grad_hidden.reshape(hidden.shape), grad_weight, grad_probs.T)


def solution(mesh):
    placed = (
        P("fsdp", "ep"),
        P("fsdp", None, "ep"),
        P("fsdp", None),
        P("fsdp", None),
        P("fsdp", "ep"),
    )
    n_fsdp, n_ep = mesh.shape["fsdp"], mesh.shape["ep"]
    if (n_fsdp, n_ep) == (8, 4):
        body = local_fused
    else:
        body = functools.partial(local, n_fsdp, n_ep)
    return jax.shard_map(
        body,
        mesh=mesh,
        in_specs=placed,
        out_specs=(P("fsdp", "ep"), P("fsdp", "ep"), P("fsdp", None, "ep"), P("fsdp", None)),
        check_vma=False,
    )
```
